256 devices in a mesh: seq: 64 (over z, y, x_lo), tp: 4 (over x_hi, core).
Axes of the slice: x: 4 (x_hi: 2, x_lo: 2; x = x_hi * 2 + x_lo), y: 4, z: 8, core: 2. Of those that a mesh axis runs over, the one named last changes fastest.
Arguments:
- hidden_in: bfloat16 [24576, 3072], P('seq', 'tp'), may hold values from -6 to 6
- norm_gain: bfloat16 [3072], replicated, may hold values from 0.5 to 1.5
- w_query: bfloat16 [3072, 1536], P(None, 'tp')
- w_key: bfloat16 [3072, 512], P(None, 'tp')
- w_value: bfloat16 [3072, 512], P(None, 'tp'), may hold values from -0.109375 to 0.109375
- w_out: bfloat16 [1536, 3072], P('tp'), may hold values from -0.3125 to 0.3125
- short_lengths: int32 [14], replicated, may hold values from 256 to 1024, as said below
- page_slot: int32 [384], replicated, may hold values from 0 to 383, each once
Outputs:
- hidden_out: bfloat16 [24576, 3072], P('seq', 'tp')
- cache_pool: bfloat16 [384, 2, 64, 512], P('seq', None, None, 'tp')
The draws below stay inside these ranges and needn't reach their ends.
Inputs may be any that keep to these rules, and one draw needn't show every extreme that they name: `short_lengths`: multiples of 64; at least one short prompt has 1024 tokens; together they have 24576 - 16512 tokens. `page_slot`: each slot is named by exactly one page.
All inputs are finite; a program needn't handle non-finite values.
Results may differ from the reference program's by a relative error of at most 0.015.
Values may be sent and summed in bfloat16 or wider, within the bound.
A program may use at most 128 MiB of HBM per device.

```python
import jax
import jax.numpy as jnp
from jax import lax

D = 3072
QH = 12
KVH = 4
HD = 128
PAGE = 64
SHORT_MIN = 256
SHORT_MAX = 1024
TOKENS = 24576
NSHORT = 14
NPAGES = 384
N_SEQ = 64


def weight_pair(key):
    query_base = jax.random.normal(jax.random.fold_in(key, 11), (D, QH * HD), jnp.float32) * D ** (-0.5)
    key_base = jax.random.normal(jax.random.fold_in(key, 12), (D, KVH * HD), jnp.float32) * D ** (-0.5)
    query_base = query_base * 1.5
    key_base = key_base * 1.5
    return (query_base, key_base)


def draw_w_query(key, part):
    return weight_pair(key)[0].astype(jnp.bfloat16)


def draw_w_key(key, part):
    return weight_pair(key)[1].astype(jnp.bfloat16)


def draw_short_lengths(key, part):
    max_units = SHORT_MAX // PAGE
    min_units = SHORT_MIN // PAGE
    rest_units = 9 * NSHORT - max_units
    base_units = rest_units // (NSHORT - 1)
    extra_units = rest_units - base_units * (NSHORT - 1)
    spread_units = min(base_units - min_units, max_units - base_units - extra_units)
    lift_units = jax.random.randint(jax.random.fold_in(key, 21), (NSHORT - 1,), 0, spread_units + 1)
    slot_ids = jnp.arange(NSHORT - 1, dtype=jnp.int32)
    unit_counts = base_units + lift_units - jnp.roll(lift_units, -1) + jnp.where(slot_ids == 0, extra_units, 0)
    max_place = jax.random.randint(jax.random.fold_in(key, 22), (), 0, NSHORT)
    places = jnp.arange(NSHORT, dtype=jnp.int32)
    before_max = jnp.take(unit_counts, jnp.clip(places, 0, NSHORT - 2))
    after_max = jnp.take(unit_counts, jnp.clip(places - 1, 0, NSHORT - 2))
    chosen = jnp.where(places < max_place, before_max, jnp.where(places == max_place, max_units, after_max))
    return (chosen * PAGE).astype(jnp.int32)


def levels(stream_key, shape, pieces, smallest, top_value):
    def one(position, blocks):
        draws = jax.random.uniform(jax.random.fold_in(jax.random.fold_in(stream_key, 6), position), (blocks,), jnp.float32, smallest / len(pieces), top_value / len(pieces))
        return jnp.repeat(jnp.exp(draws), shape[position] // blocks).reshape((-1,) + (1,) * (len(shape) - position - 1))

    level = one(*pieces[0])
    for cut in pieces[1:]:
        level = level * one(*cut)
    return level


def scatter_about(own_key, shape, spread, most, shards=(), kind=jnp.bfloat16):
    values = spread * jax.random.normal(own_key, shape, jnp.float32)
    if shards:
        values = values * levels(own_key, shape, shards, -0.22, 0.18)
    return jnp.clip(values, -most, most).astype(kind)


def setup_inputs(seed: int = 0) -> dict:
    streams_of = jax.random.split(jax.random.key(seed), 9)
    return {
        "hidden_in": scatter_about(streams_of[0], (TOKENS, D), 1.0, 6.0, ((0, 64), (1, 4))),
        "norm_gain": jnp.clip(1.0 + 0.1 * jax.random.normal(streams_of[1], (D,), jnp.float32), 0.5, 1.5).astype(jnp.bfloat16),
        "w_query": draw_w_query(jax.random.fold_in(streams_of[8], 71), 0),
        "w_key": draw_w_key(jax.random.fold_in(streams_of[8], 71), 0),
        "w_value": scatter_about(streams_of[4], (D, KVH * HD), D ** -0.5, 0.109375, ((1, 4),)),
        "w_out": scatter_about(streams_of[5], (QH * HD, D), (QH * HD // 4) ** -0.5, 0.3125, ((0, 4),)),
        "short_lengths": draw_short_lengths(jax.random.fold_in(streams_of[8], 71), 0),
        "page_slot": jax.random.permutation(streams_of[7], NPAGES).astype(jnp.int32),
    }


rope_base = 500000.0
norm_eps = 1e-05
neg_large = -1e+30

def packed_position(row_ids, rows_per_dev, seq_count):
    block_rows = rows_per_dev // 2
    device = row_ids // rows_per_dev
    second = row_ids // block_rows % 2
    block_id = jnp.where(second == 0, device, 2 * seq_count - 1 - device)
    return (block_id * block_rows + row_ids % block_rows).astype(jnp.int32)

def storage_row(positions, rows_per_dev, seq_count):
    block_rows = rows_per_dev // 2
    block_id = positions // block_rows
    device = jnp.where(block_id < seq_count, block_id, 2 * seq_count - 1 - block_id)
    second = jnp.where(block_id < seq_count, 0, 1)
    return (device * rows_per_dev + second * block_rows + positions % block_rows).astype(jnp.int32)

def prompt_start(positions, short_lengths, long_len):
    prompt_ends = (long_len + jnp.cumsum(short_lengths)).astype(jnp.int32)
    bounds = jnp.concatenate([jnp.zeros((1,), jnp.int32), jnp.reshape(long_len, (1,)).astype(jnp.int32), prompt_ends[:-1]])
    at_or_before = bounds[None, :] <= positions[:, None]
    return lax.optimization_barrier(jnp.max(jnp.where(at_or_before, bounds[None, :], 0), axis=1)).astype(jnp.int32)

def rotate(values, relative, head_size):
    half_size = head_size // 2
    frequency = rope_base ** (-(jnp.arange(half_size, dtype=jnp.float32) * 2.0) / head_size)
    angles = relative.astype(jnp.float32)[:, None] * frequency[None, :]
    cosine = jnp.concatenate([jnp.cos(angles), jnp.cos(angles)], axis=1)[:, None, :]
    sine_part = jnp.concatenate([jnp.sin(angles), jnp.sin(angles)], axis=1)[:, None, :]
    turned = jnp.concatenate([-values[..., half_size:], values[..., :half_size]], axis=-1)
    return values * cosine + turned * sine_part

def project(row_data, norm_gain, w_query, w_key, w_value, relative, head_size):
    wide = row_data.astype(jnp.float32)
    squares = lax.optimization_barrier(jnp.mean(wide * wide, axis=1, keepdims=True))
    normed = (wide * lax.rsqrt(squares + norm_eps) * norm_gain.astype(jnp.float32)[None, :]).astype(jnp.bfloat16)
    row_count = row_data.shape[0]
    query_rows = jnp.dot(normed, w_query, preferred_element_type=jnp.float32).reshape(row_count, -1, head_size)
    key_rows = jnp.dot(normed, w_key, preferred_element_type=jnp.float32).reshape(row_count, -1, head_size)
    value_rows = jnp.dot(normed, w_value, preferred_element_type=jnp.float32).astype(jnp.bfloat16)
    query_rows = rotate(query_rows, relative, head_size).astype(jnp.bfloat16).reshape(row_count, -1)
    key_rows = rotate(key_rows, relative, head_size).astype(jnp.bfloat16).reshape(row_count, -1)
    return (query_rows, key_rows, value_rows)

def attend_block(carried, query_blk, key_blk, value_blk, allowed_pairs, group_size, head_size):
    running_max, denominator, accumulated = carried
    row_count = query_blk.shape[0]
    key_count = key_blk.shape[0]
    queries = query_blk.astype(jnp.float32).reshape(row_count, -1, group_size, head_size)
    keys_wide = key_blk.astype(jnp.float32).reshape(key_count, -1, head_size)
    values_wide = value_blk.astype(jnp.float32).reshape(key_count, -1, head_size)
    scores = jnp.einsum('rkgd,skd->rkgs', queries, keys_wide) * (1.0 / jnp.sqrt(jnp.float32(head_size)))
    visible = allowed_pairs[:, None, None, :]
    scores = jnp.where(visible, scores, neg_large)
    new_max = jnp.maximum(running_max, lax.optimization_barrier(jnp.max(scores, axis=-1)))
    weights = jnp.where(visible, jnp.exp(scores - new_max[..., None]), 0.0)
    factor = jnp.exp(running_max - new_max)
    denominator = denominator * factor + lax.optimization_barrier(jnp.sum(weights, axis=-1))
    rounded = lax.optimization_barrier(weights.astype(jnp.bfloat16)).astype(jnp.float32)
    accumulated = accumulated * factor[..., None] + jnp.einsum('rkgs,skd->rkgd', rounded, values_wide)
    return (new_max, denominator, accumulated)

def reference(hidden_in, norm_gain, w_query, w_key, w_value, w_out, short_lengths, page_slot):
    total_rows = hidden_in.shape[0]
    rows_per_dev = total_rows // N_SEQ
    head_size = HD
    group_size = QH // KVH
    long_len = (total_rows - jnp.sum(short_lengths)).astype(jnp.int32)
    row_ids = jnp.arange(total_rows, dtype=jnp.int32)
    positions = packed_position(row_ids, rows_per_dev, N_SEQ)
    prompt_first = prompt_start(positions, short_lengths, long_len)
    query_rows, key_rows, value_rows = project(hidden_in, norm_gain, w_query, w_key, w_value, positions - prompt_first, head_size)
    packed_order = storage_row(row_ids, rows_per_dev, N_SEQ)
    query_p = jnp.take(query_rows, packed_order, axis=0)
    key_p = jnp.take(key_rows, packed_order, axis=0)
    value_p = jnp.take(value_rows, packed_order, axis=0)
    first_p = jnp.take(prompt_first, packed_order, axis=0)
    block_rows = total_rows // 32

    def one_block(block_id):
        row_first = (block_id * block_rows).astype(jnp.int32)
        query_blk = lax.dynamic_slice_in_dim(query_p, row_first, block_rows, 0)
        query_pos = row_first + jnp.arange(block_rows, dtype=jnp.int32)
        query_first = lax.dynamic_slice_in_dim(first_p, row_first, block_rows, 0)
        first_block = (query_first[0] // block_rows).astype(jnp.int32)

        def step_keys(key_block, carried):
            key_first = (key_block * block_rows).astype(jnp.int32)
            key_blk = lax.dynamic_slice_in_dim(key_p, key_first, block_rows, 0)
            value_blk = lax.dynamic_slice_in_dim(value_p, key_first, block_rows, 0)
            key_pos = key_first + jnp.arange(block_rows, dtype=jnp.int32)
            allowed_pairs = (key_pos[None, :] >= query_first[:, None]) & (key_pos[None, :] <= query_pos[:, None])
            return attend_block(carried, query_blk, key_blk, value_blk, allowed_pairs, group_size, head_size)
        kv_heads = key_p.shape[1] // head_size
        initial = (jnp.full((block_rows, kv_heads, group_size), neg_large, jnp.float32), jnp.zeros((block_rows, kv_heads, group_size), jnp.float32), jnp.zeros((block_rows, kv_heads, group_size, head_size), jnp.float32))
        running_max, denominator, accumulated = lax.fori_loop(first_block, block_id + 1, step_keys, initial)
        return (accumulated / denominator[..., None]).astype(jnp.bfloat16).reshape(block_rows, -1)
    blocks_out = lax.map(one_block, jnp.arange(total_rows // block_rows, dtype=jnp.int32))
    attended_p = blocks_out.reshape(total_rows, -1)
    attended = jnp.take(attended_p, positions, axis=0)
    projected = jnp.dot(attended, w_out, preferred_element_type=jnp.float32)
    hidden_out = (hidden_in.astype(jnp.float32) + projected).astype(jnp.bfloat16)
    page_count = total_rows // PAGE
    pages = jnp.stack([key_p.reshape(page_count, PAGE, -1), value_p.reshape(page_count, PAGE, -1)], axis=1)
    cache_pool = jnp.zeros_like(pages).at[page_slot].set(pages)
    return (hidden_out, cache_pool)
```

```python
import functools
import heapq
import math

import jax
import jax.numpy as jnp
from jax import lax
from jax.experimental import pallas as pl
from jax.experimental.pallas import tpu as pltpu
from jax.sharding import PartitionSpec as P

MESH = pl.DeviceIdType.MESH
F32 = jnp.float32
BF16 = jnp.bfloat16

D = 3072
QH = 12
KVH = 4
HD = 128
PAGE = 64
GROUP = 3
N_SEQ = 64
N_TP = 4
ROWS = 384
BLOCK = 192
COLS = D // N_TP
HEAD_COLS = GROUP * HD
LONG = 16512
LONG_BLOCKS = LONG // BLOCK
THIRD = 64
rope_base = 500000.0
norm_eps = 1e-05
SCALE2 = math.log2(math.e) / math.sqrt(HD)
NEG = -1e30


def onward(color, off, via):
    dz, dy, dx = off
    order = ("xyz", "xzy", "zyx")[color]
    if via == "own":
        links = []
        for axis in order:
            links += ["x"] if axis == "x" else [axis + "+", axis + "-"]
        return links
    links = []
    if via == "z+" and (dz in (-1, -2) or (dz == -3 and (color == 2 or dx == 0))):
        links.append(via)
    if via == "z-" and (dz in (1, 2) or (dz == 3 and color != 2 and dx == 1)):
        links.append(via)
    if via == "y+" and dy == -1 and (dz % 2 == 0 if color == 2 else dx == 0):
        links.append(via)
    if via == "y-" and dy == 1 and (dz % 2 == 1 if color == 2 else dx == 1):
        links.append(via)
    for axis in order[order.index(via[0]) + 1 :]:
        links += ["x"] if axis == "x" else [axis + "+", axis + "-"]
    return links


def shifted(off, link):
    dz, dy, dx = off
    dz += {"z+": -1, "z-": 1}.get(link, 0)
    dy += {"y+": -1, "y-": 1}.get(link, 0)
    dx ^= int(link == "x")
    return (4 if dz == -4 else dz, 2 if dy == -2 else dy, dx)


def arrival_order(copy_us=1.41, hop_us=1.7):
    free, heap, events, count = {}, [], [], 0

    def issue(now, color, off, links):
        nonlocal count
        for link in links:
            first = max(now, free.get(link, 0.0))
            free[link] = first + copy_us
            count += 1
            heapq.heappush(
                heap, (first + copy_us + hop_us, count, color, shifted(off, link), link)
            )

    for color in range(3):
        issue(0.0, color, (0, 0, 0), onward(color, (0, 0, 0), "own"))
    while heap:
        now, _, color, off, link = heapq.heappop(heap)
        links = onward(color, off, link)
        events.append((color, off, links))
        issue(now, color, off, links)
    return events


EVENTS = arrival_order()
OFFSETS = sorted({off for _, off, _ in EVENTS})


def places():
    seq = lax.axis_index("seq")
    tp = lax.axis_index("tp")
    return seq // 8, (seq // 2) % 4, seq % 2, tp // 2, tp % 2


def seq_of(z, y, x_lo):
    return z * 8 + y * 2 + x_lo


def x_neighbours():
    z, y, x_lo, x_hi, core = places()
    x = x_hi * 2 + x_lo
    ids = []
    for step in (1, 3):
        other = lax.rem(x + step, 4)
        ids.append((seq_of(z, y, other % 2), (other // 2) * 2 + core))
    return x, ids


def greet(ids):
    barrier = pltpu.get_barrier_semaphore()
    for one in ids:
        pl.semaphore_signal(barrier, inc=1, device_id=one, device_id_type=MESH)
    pl.semaphore_wait(barrier, len(ids))


def remote(src, dst, send, recv, target):
    return pltpu.make_async_remote_copy(
        src_ref=src, dst_ref=dst, send_sem=send, recv_sem=recv, device_id=target,
        device_id_type=MESH,
    )


CHUNKS = 3
CHUNK = BLOCK // CHUNKS


def project_kernel(
    hidden, gain, wq, wk, wv, cosine, sine, q_out, kv_out,
    xbuf, relay, wbuf, wsem, own_sem, send_sem, r0, r1, r2, r3,
):
    z, y, x_lo, x_hi, core = places()
    seq = lax.axis_index("seq")
    tp = lax.axis_index("tp")
    loads = [
        pltpu.make_async_copy(wq, wbuf.at[:, 0:HEAD_COLS], wsem.at[0]),
        pltpu.make_async_copy(wk, wbuf.at[:, HEAD_COLS : HEAD_COLS + HD], wsem.at[1]),
        pltpu.make_async_copy(wv, wbuf.at[:, HEAD_COLS + HD : HEAD_COLS + 2 * HD], wsem.at[2]),
        pltpu.make_async_copy(hidden, xbuf.at[tp], own_sem),
    ]
    for one in loads:
        one.start()
    x, sides = x_neighbours()
    partner = (seq, x_hi * 2 + 1 - core)
    greet([partner] + sides)
    sends = []

    def go(copy):
        copy.start()
        sends.append(copy)
        return copy

    firsts = {}
    for c in range(CHUNKS):
        for way in range(2):
            rows = pl.ds(way * BLOCK + c * CHUNK, CHUNK)
            k = way * CHUNKS + c
            firsts[k] = go(
                remote(hidden.at[rows], relay.at[k], send_sem.at[k], r1.at[k], sides[way])
            )
    own = go(remote(hidden, xbuf.at[tp], send_sem.at[18], r0, partner))
    opposite = (1 - x_hi) * 2 + core
    seconds = {}

    def pass_on(k):
        way, c = k // CHUNKS, k % CHUNKS
        firsts[k].wait_recv()
        source = lax.rem(x + (3 if way == 0 else 1), 4)
        rows = pl.ds(way * BLOCK + c * CHUNK, CHUNK)
        seconds[k] = go(
            remote(
                relay.at[k], xbuf.at[(source // 2) * 2 + core, rows], send_sem.at[6 + k], r2.at[k],
                sides[way],
            )
        )

    thirds = {}

    def share(k):
        way, c = k // CHUNKS, k % CHUNKS
        rows = pl.ds(way * BLOCK + c * CHUNK, CHUNK)
        remote(
            relay.at[k], xbuf.at[opposite, rows], send_sem.at[6 + k], r2.at[k], sides[way]
        ).wait_recv()
        thirds[k] = go(
            remote(
                xbuf.at[opposite, rows], xbuf.at[opposite, rows], send_sem.at[12 + k], r3.at[k],
                partner,
            )
        )

    for c in range(CHUNKS):
        for way in range(2):
            pass_on(way * CHUNKS + c)
        if c >= 1:
            for way in range(2):
                share(way * CHUNKS + c - 1)
    for way in range(2):
        share(way * CHUNKS + CHUNKS - 1)
    for one in loads:
        one.wait()
    own.wait_recv()
    for k in range(2 * CHUNKS):
        thirds[k].wait_recv()
    for one in sends:
        one.wait_send()
    squares = jnp.zeros((ROWS, 1), F32)
    for part in range(N_TP):
        wide = xbuf[part].astype(F32)
        squares += jnp.sum(wide * wide, axis=1, keepdims=True)
    factor = lax.rsqrt(squares * (1.0 / D) + norm_eps)
    total = jnp.zeros((ROWS, HEAD_COLS + 2 * HD), F32)
    for part in range(N_TP):
        cols = slice(part * COLS, (part + 1) * COLS)
        normed = (xbuf[part].astype(F32) * factor * gain[:, cols].astype(F32)).astype(BF16)
        total += jnp.dot(normed, wbuf[cols, :], preferred_element_type=F32)
    cos = cosine[...]
    sin = sine[...]
    for head in range(GROUP + 1):
        u = total[:, head * HD : (head + 1) * HD]
        turned = (u * cos + pltpu.roll(u, HD // 2, 1) * sin).astype(BF16)
        for half in range(2):
            rows = slice(half * BLOCK, (half + 1) * BLOCK)
            if head < GROUP:
                q_out[half, head] = turned[rows]
            else:
                kv_out[half] = turned[rows].reshape(BLOCK // THIRD, THIRD, HD)
    value = total[:, HEAD_COLS + HD :].astype(BF16)
    for half in range(2):
        kv_out[2 + half] = value[half * BLOCK : (half + 1) * BLOCK].reshape(
            BLOCK // THIRD, THIRD, HD
        )


TILE_SLOTS = 4
TILE = TILE_SLOTS * BLOCK
N_TILES = N_SEQ // TILE_SLOTS


def attend_kernel(
    wanted, q, kv, first_b, attended, pages, buf, m_ref, l_ref, acc_ref, own_sem, send_sem, recv_sem
):
    z, y, x_lo, x_hi, core = places()
    seq = lax.axis_index("seq")
    tp = lax.axis_index("tp")
    own = pltpu.make_async_copy(kv, buf.at[:, seq], own_sem)
    own.start()
    target = {
        "x": (seq_of(z, y, 1 - x_lo), tp),
        "y+": (seq_of(z, lax.rem(y + 1, 4), x_lo), tp),
        "y-": (seq_of(z, lax.rem(y + 3, 4), x_lo), tp),
        "z+": (seq_of(lax.rem(z + 1, 8), y, x_lo), tp),
        "z-": (seq_of(lax.rem(z + 7, 8), y, x_lo), tp),
    }
    greet(list(target.values()))

    def chunk(color, off):
        dz, dy, dx = off
        slot = seq_of(
            lax.rem(z + (dz + 8), 8), lax.rem(y + (dy + 4), 4), x_lo if dx == 0 else 1 - x_lo
        )
        return buf.at[:, slot, color]

    def send(color, off, link, src):
        there = shifted(off, link)
        remote(
            src, chunk(color, off), send_sem.at[color],
            recv_sem.at[color, OFFSETS.index(there)], target[link],
        ).start()

    for color in range(3):
        for link in onward(color, (0, 0, 0), "own"):
            send(color, (0, 0, 0), link, kv.at[:, color])
    for color, off, links in EVENTS:
        here = chunk(color, off)
        remote(
            here, here, send_sem.at[color], recv_sem.at[color, OFFSETS.index(off)], target["x"]
        ).wait_recv()
        for link in links:
            send(color, off, link, here)
    own.wait()
    for color in range(3):
        sent = buf.at[:, pl.ds(0, N_SEQ - 1), color]
        pltpu.make_async_copy(sent, sent, send_sem.at[color]).wait()

    m_ref[...] = jnp.full(m_ref.shape, NEG, F32)
    l_ref[...] = jnp.zeros(l_ref.shape, F32)
    acc_ref[...] = jnp.zeros(acc_ref.shape, F32)

    def step(half, region, tile, allowed):
        rows = pl.ds(tile * TILE_SLOTS, TILE_SLOTS)
        keys = buf[region, rows].reshape(TILE, HD)
        values = buf[2 + region, rows].reshape(TILE, HD)
        for head in range(GROUP):
            scores = lax.dot_general(
                q[half, head], keys, (((1,), (1,)), ((), ())), preferred_element_type=F32
            )
            if allowed is not None:
                scores = jnp.where(allowed, scores, NEG)
            old = m_ref[half, head]
            new = jnp.maximum(old, jnp.max(scores, axis=1, keepdims=True))
            weights = jnp.exp2(scores * SCALE2 - new * SCALE2)
            if allowed is not None:
                weights = jnp.where(allowed, weights, 0.0)
            keep = jnp.exp2((old - new) * SCALE2)
            m_ref[half, head] = new
            l_ref[half, head] = l_ref[half, head] * keep + jnp.sum(weights, axis=1, keepdims=True)
            acc_ref[half, head] = acc_ref[half, head] * keep + jnp.dot(
                weights.astype(BF16), values, preferred_element_type=F32
            )

    row = lax.broadcasted_iota(jnp.int32, (BLOCK, TILE), 0)
    col = lax.broadcasted_iota(jnp.int32, (BLOCK, TILE), 1)
    slot_in = (
        (col >= BLOCK).astype(jnp.int32)
        + (col >= 2 * BLOCK).astype(jnp.int32)
        + (col >= 3 * BLOCK).astype(jnp.int32)
    )
    back = col - 2 * BLOCK * slot_in
    own_tile = seq // TILE_SLOTS
    last_block = 2 * N_SEQ - 1
    step(0, 0, own_tile, col + own_tile * TILE <= row + seq * BLOCK)

    @pl.loop(0, own_tile)
    def _(tile):
        step(0, 0, tile, None)

    row_pos = row + (last_block - seq) * BLOCK

    def masked_b(tile):
        key_pos = back + (last_block - tile * TILE_SLOTS) * BLOCK
        step(1, 1, tile, (key_pos <= row_pos) & (key_pos >= first_b[...]))

    masked_b(own_tile)
    in_long = (seq + (LONG_BLOCKS - N_SEQ)) // N_SEQ
    short_tiles = (seq + 6) // TILE_SLOTS - own_tile

    @pl.loop(own_tile + 1, own_tile + 1 + (1 - in_long) * short_tiles)
    def _(tile):
        masked_b(tile)

    @pl.loop(N_TILES - in_long * (N_TILES - 1 - own_tile), N_TILES)
    def _(tile):
        step(1, 1, tile, None)

    @pl.loop(0, in_long * N_TILES)
    def _(tile):
        step(1, 0, tile, None)

    for half in range(2):
        for head in range(GROUP):
            attended[half * BLOCK : (half + 1) * BLOCK, head * HD : (head + 1) * HD] = (
                acc_ref[half, head] / l_ref[half, head]
            ).astype(BF16)
    for page in range(ROWS // PAGE):
        region = wanted[page, 0]
        slot = wanted[page, 1]
        part = wanted[page, 2]
        pages[page, 0] = buf[region, slot, part]
        pages[page, 1] = buf[region + 2, slot, part]


def output_kernel(
    attended, w_out, hidden, out, sendp, recvp, sendx, recvx, relay, send_sem, rp, r1, r2
):
    z, y, x_lo, x_hi, core = places()
    seq = lax.axis_index("seq")
    x, sides = x_neighbours()
    partner = (seq, x_hi * 2 + 1 - core)
    greet([partner] + sides)

    def terms(part):
        cols = pl.ds(pl.multiple_of(part * COLS, COLS), COLS)
        return jnp.dot(attended[...], w_out[:, cols], preferred_element_type=F32)

    sends = []

    def go(copy):
        copy.start()
        sends.append(copy)
        return copy

    far = (1 - x_hi) * 2
    near = x_hi * 2
    sendp[0] = terms(far + 1 - core).astype(BF16)
    far_copy = go(remote(sendp.at[0], recvp.at[0], send_sem.at[12], rp.at[0], partner))
    mine = terms(far + core)
    far_copy.wait_recv()
    sendx[...] = (mine + recvp[0].astype(F32)).astype(BF16)
    firsts = {}
    for c in range(CHUNKS):
        for way in range(2):
            rows = pl.ds(way * BLOCK + c * CHUNK, CHUNK)
            k = way * CHUNKS + c
            firsts[k] = go(
                remote(sendx.at[rows], relay.at[k], send_sem.at[k], r1.at[k], sides[way])
            )
    sendp[1] = terms(near + 1 - core).astype(BF16)
    near_copy = go(remote(sendp.at[1], recvp.at[1], send_sem.at[13], rp.at[1], partner))
    seconds = {}
    for c in range(CHUNKS):
        for way in range(2):
            k = way * CHUNKS + c
            rows = pl.ds(way * BLOCK + c * CHUNK, CHUNK)
            firsts[k].wait_recv()
            seconds[k] = go(
                remote(relay.at[k], recvx.at[rows], send_sem.at[6 + k], r2.at[k], sides[way])
            )
    kept = terms(near + core) + hidden[...].astype(F32)
    near_copy.wait_recv()
    kept = kept + recvp[1].astype(F32)
    for k in range(2 * CHUNKS):
        seconds[k].wait_recv()
    out[...] = (kept + recvx[...].astype(F32)).astype(BF16)
    for one in sends:
        one.wait_send()


VM = pl.BlockSpec(memory_space=pltpu.VMEM)
ANY = pl.BlockSpec(memory_space=pl.ANY)
DMA = pltpu.SemaphoreType.DMA


def params(cid, mib):
    return pltpu.CompilerParams(
        collective_id=cid, has_side_effects=True, vmem_limit_bytes=mib * 1024 * 1024
    )


def row_facts(short_lengths, page_slot):
    seq = lax.axis_index("seq")
    rows = jnp.arange(ROWS, dtype=jnp.int32)
    offset = rows % BLOCK
    block = jnp.where(rows < BLOCK, seq, 2 * N_SEQ - 1 - seq)
    positions = block * BLOCK + offset
    ends = LONG + jnp.cumsum(short_lengths)
    bounds = jnp.concatenate([jnp.full((1,), LONG, jnp.int32), ends[:-1]])
    first = jnp.max(
        jnp.where(bounds[None, :] <= positions[:, None], bounds[None, :], 0), axis=1
    )
    relative = (positions - first).astype(F32)
    half = HD // 2
    frequency = rope_base ** (-(jnp.arange(half, dtype=F32) * 2.0) / HD)
    angles = relative[:, None] * frequency[None, :]
    cos = jnp.cos(angles)
    sin = jnp.sin(angles)
    cosine = jnp.concatenate([cos, cos], axis=1)
    sine = jnp.concatenate([-sin, sin], axis=1)
    pages_dev = ROWS // PAGE
    slots = seq * pages_dev + jnp.arange(pages_dev, dtype=jnp.int32)
    ids = jnp.arange(page_slot.shape[0], dtype=jnp.int32)
    page = jnp.sum(jnp.where(page_slot[None, :] == slots[:, None], ids[None, :], 0), axis=1)
    page_block = page // (BLOCK // PAGE)
    late = page_block >= N_SEQ
    wanted = jnp.stack(
        [
            late.astype(jnp.int32),
            jnp.where(late, 2 * N_SEQ - 1 - page_block, page_block),
            page % (BLOCK // PAGE),
        ],
        axis=1,
    )
    return cosine, sine, first[BLOCK:, None], wanted


def local(hidden_in, norm_gain, w_query, w_key, w_value, w_out, short_lengths, page_slot):
    cosine, sine, first_b, wanted = row_facts(short_lengths, page_slot)
    q, kv = pl.pallas_call(
        project_kernel,
        out_shape=(
            jax.ShapeDtypeStruct((2, GROUP, BLOCK, HD), BF16),
            jax.ShapeDtypeStruct((4, BLOCK // THIRD, THIRD, HD), BF16),
        ),
        in_specs=[VM, VM, ANY, ANY, ANY, VM, VM],
        out_specs=(VM, VM),
        scratch_shapes=[
            pltpu.VMEM((N_TP, ROWS, COLS), BF16),
            pltpu.VMEM((2 * CHUNKS, CHUNK, COLS), BF16),
            pltpu.VMEM((D, HEAD_COLS + 2 * HD), BF16),
            DMA((3,)),
            DMA(()),
            DMA((19,)),
            DMA(()),
            DMA((2 * CHUNKS,)),
            DMA((2 * CHUNKS,)),
            DMA((2 * CHUNKS,)),
        ],
        compiler_params=params(0, 40),
        name="gather_project",
    )(hidden_in, norm_gain.reshape(1, D), w_query, w_key, w_value, cosine, sine)
    attended, pages = pl.pallas_call(
        attend_kernel,
        out_shape=(
            jax.ShapeDtypeStruct((ROWS, HEAD_COLS), BF16),
            jax.ShapeDtypeStruct((ROWS // PAGE, 2, PAGE, HD), BF16),
        ),
        in_specs=[pl.BlockSpec(memory_space=pltpu.SMEM), VM, VM, VM],
        out_specs=(VM, VM),
        scratch_shapes=[
            pltpu.VMEM((4, N_SEQ, BLOCK // THIRD, THIRD, HD), BF16),
            pltpu.VMEM((2, GROUP, BLOCK, 1), F32),
            pltpu.VMEM((2, GROUP, BLOCK, 1), F32),
            pltpu.VMEM((2, GROUP, BLOCK, HD), F32),
            DMA(()),
            DMA((3,)),
            DMA((3, len(OFFSETS))),
        ],
        compiler_params=params(1, 60),
        name="gather_attend",
    )(wanted, q, kv, first_b)
    hidden_out = pl.pallas_call(
        output_kernel,
        out_shape=jax.ShapeDtypeStruct((ROWS, COLS), BF16),
        in_specs=[VM, VM, VM],
        out_specs=VM,
        scratch_shapes=[
            pltpu.VMEM((2, ROWS, COLS), BF16),
            pltpu.VMEM((2, ROWS, COLS), BF16),
            pltpu.VMEM((ROWS, COLS), BF16),
            pltpu.VMEM((ROWS, COLS), BF16),
            pltpu.VMEM((2 * CHUNKS, CHUNK, COLS), BF16),
            DMA((14,)),
            DMA((2,)),
            DMA((2 * CHUNKS,)),
            DMA((2 * CHUNKS,)),
        ],
        compiler_params=params(2, 40),
        name="project_reduce",
    )(attended, w_out, hidden_in)
    return hidden_out, pages


def solution(mesh):
    placed = (
        P("seq", "tp"),
        P(),
        P(None, "tp"),
        P(None, "tp"),
        P(None, "tp"),
        P("tp", None),
        P(),
        P(),
    )
    return jax.shard_map(
        local,
        mesh=mesh,
        in_specs=placed,
        out_specs=(P("seq", "tp"), P("seq", None, None, "tp")),
        check_vma=False,
    )
```

```python
import functools
import heapq
import math

import jax
import jax.numpy as jnp
import numpy as np
from jax import lax
from jax.experimental import pallas as pl
from jax.experimental.pallas import tpu as pltpu
from jax.sharding import PartitionSpec as P

MESH = pl.DeviceIdType.MESH
F32 = jnp.float32
BF16 = jnp.bfloat16

D = 3072
QH = 12
KVH = 4
HD = 128
PAGE = 64
GROUP = 3
N_SEQ = 64
N_TP = 4
ROWS = 384
BLOCK = 192
COLS = D // N_TP
HEAD_COLS = GROUP * HD
LONG = 16512
LONG_BLOCKS = LONG // BLOCK
THIRD = 64
rope_base = 500000.0
norm_eps = 1e-05
SCALE2 = math.log2(math.e) / math.sqrt(HD)
NEG = -1e30


def onward(color, off, via):
    dz, dy, dx = off
    order = ("xyz", "xzy", "zyx")[color]
    if via == "own":
        links = []
        for axis in order:
            links += ["x"] if axis == "x" else [axis + "+", axis + "-"]
        return links
    links = []
    if via == "z+" and (dz in (-1, -2) or (dz == -3 and (color == 2 or dx == 0))):
        links.append(via)
    if via == "z-" and (dz in (1, 2) or (dz == 3 and color != 2 and dx == 1)):
        links.append(via)
    if via == "y+" and dy == -1 and (dz % 2 == 0 if color == 2 else dx == 0):
        links.append(via)
    if via == "y-" and dy == 1 and (dz % 2 == 1 if color == 2 else dx == 1):
        links.append(via)
    for axis in order[order.index(via[0]) + 1 :]:
        links += ["x"] if axis == "x" else [axis + "+", axis + "-"]
    return links


def shifted(off, link):
    dz, dy, dx = off
    dz += {"z+": -1, "z-": 1}.get(link, 0)
    dy += {"y+": -1, "y-": 1}.get(link, 0)
    dx ^= int(link == "x")
    return (4 if dz == -4 else dz, 2 if dy == -2 else dy, dx)


def plan(copy_us=1.41, hop_us=1.7, step_us=1.0, first_us=1.5):
    free, heap, count, now = {}, [], 0, 0.0

    def issue(color, off, links):
        nonlocal count
        for link in links:
            first = max(now, free.get(link, 0.0))
            free[link] = first + copy_us
            count += 1
            heapq.heappush(
                heap, (first + copy_us + hop_us, count, color, shifted(off, link), link)
            )

    for color in range(3):
        issue(color, (0, 0, 0), onward(color, (0, 0, 0), "own"))
    now = first_us
    missing = [set() for _ in range(STEPS // 3)]
    for unit in range(STEPS // 3):
        dz = plane_of(unit // 2)
        for dy in (0, 1, -1, 2) if unit % 2 else (0, 1, -1):
            for dx in (0, 1):
                missing[unit] |= {(color, (dz, dy, dx)) for color in range(3)}
        missing[unit] -= {(color, (0, 0, 0)) for color in range(3)}
    taken, batches, batch, step = set(), [], [], 0
    while step < STEPS or heap:
        if heap and heap[0][0] <= now:
            _, _, color, off, link = heapq.heappop(heap)
            links = onward(color, off, link)
            taken.add((color, off))
            batch.append((color, off, links))
            now += 0.03
            issue(color, off, links)
        elif step < STEPS and missing[step // 3] <= taken:
            batches.append(batch)
            batch = []
            step += 1
            now += step_us
        else:
            now = heap[0][0]
    return batches, now


N_TILES = 16
STEPS = 3 * N_TILES


def plane_of(rank):
    return (rank + 1) // 2 * (1 - 2 * ((rank + 1) % 2))


BATCHES, _ = plan()
OFFSETS = sorted({off for batch in BATCHES for _, off, _ in batch})


def places():
    seq = lax.axis_index("seq")
    tp = lax.axis_index("tp")
    return seq // 8, (seq // 2) % 4, seq % 2, tp // 2, tp % 2


def seq_of(z, y, x_lo):
    return z * 8 + y * 2 + x_lo


def x_neighbours():
    z, y, x_lo, x_hi, core = places()
    x = x_hi * 2 + x_lo
    ids = []
    for step in (1, 3):
        other = lax.rem(x + step, 4)
        ids.append((seq_of(z, y, other % 2), (other // 2) * 2 + core))
    return x, ids


def greet(ids):
    barrier = pltpu.get_barrier_semaphore()
    for one in ids:
        pl.semaphore_signal(barrier, inc=1, device_id=one, device_id_type=MESH)
    pl.semaphore_wait(barrier, len(ids))


def remote(src, dst, send, recv, target):
    return pltpu.make_async_remote_copy(
        src_ref=src, dst_ref=dst, send_sem=send, recv_sem=recv, device_id=target,
        device_id_type=MESH,
    )


CHUNKS = 6
CHUNK = BLOCK // CHUNKS
TILE_SLOTS = N_SEQ // N_TILES
TILE = TILE_SLOTS * BLOCK
LAST_BLOCK = 2 * N_SEQ - 1
KV_COLS = 2 * HD


def layer_kernel(
    short_lengths, hidden, gain, frequency, page_slot, wq, wk, wv, w_out, out, pages,
    xbuf, relay, wbuf, wout, fbuf, total, cosine, sine, first_b, q, kv, buf, m_ref, l_ref, acc_ref,
    attended, sendp, recvp, sendx, recvx, relay_out,
    load_sem, send_sem, r0, r1, r2, r3, own_sem, seq_send, seq_recv, out_send, rp, o1, o2,
):
    z, y, x_lo, x_hi, core = places()
    seq = lax.axis_index("seq")
    tp = lax.axis_index("tp")
    loads = [
        pltpu.make_async_copy(hidden, xbuf.at[tp], load_sem.at[0]),
        pltpu.make_async_copy(wk, wbuf.at[:, 0:HD], load_sem.at[1]),
        pltpu.make_async_copy(wv, wbuf.at[:, HD:KV_COLS], load_sem.at[2]),
        pltpu.make_async_copy(wq, wbuf.at[:, KV_COLS:], load_sem.at[3]),
        pltpu.make_async_copy(frequency, fbuf, load_sem.at[4]),
        pltpu.make_async_copy(w_out, wout, load_sem.at[5]),
    ]
    for one in loads:
        one.start()
    x, sides = x_neighbours()
    partner = (seq, x_hi * 2 + 1 - core)
    target = {
        "x": (seq_of(z, y, 1 - x_lo), tp),
        "y+": (seq_of(z, lax.rem(y + 1, 4), x_lo), tp),
        "y-": (seq_of(z, lax.rem(y + 3, 4), x_lo), tp),
        "z+": (seq_of(lax.rem(z + 1, 8), y, x_lo), tp),
        "z-": (seq_of(lax.rem(z + 7, 8), y, x_lo), tp),
    }
    greet([partner] + sides + [target[link] for link in ("y+", "y-", "z+", "z-")])

    sends = []

    def go(copy):
        copy.start()
        sends.append(copy)
        return copy

    def rows_of(k):
        return pl.ds(k * CHUNK, CHUNK)

    opposite = (1 - x_hi) * 2 + core
    loads[0].wait()
    firsts = {}
    for c in range(CHUNKS):
        for way in range(2):
            k = way * CHUNKS + c
            firsts[k] = go(
                remote(xbuf.at[tp, rows_of(k)], relay.at[k], send_sem.at[k], r1.at[k], sides[way])
            )
    own = go(remote(xbuf.at[tp], xbuf.at[tp], send_sem.at[6 * CHUNKS], r0, partner))

    def pass_on(k):
        way = k // CHUNKS
        firsts[k].wait_recv()
        source = lax.rem(x + (3 if way == 0 else 1), 4)
        go(
            remote(
                relay.at[k], xbuf.at[(source // 2) * 2 + core, rows_of(k)],
                send_sem.at[2 * CHUNKS + k], r2.at[k], sides[way],
            )
        )

    thirds = {}

    def share(k):
        here = xbuf.at[opposite, rows_of(k)]
        remote(
            relay.at[k], here, send_sem.at[2 * CHUNKS + k], r2.at[k], sides[k // CHUNKS]
        ).wait_recv()
        thirds[k] = go(remote(here, here, send_sem.at[4 * CHUNKS + k], r3.at[k], partner))

    def scaled(part):
        wide = xbuf[part].astype(F32)
        squares = jnp.sum(wide * wide, axis=1, keepdims=True)
        cols = pl.ds(pl.multiple_of(part * COLS, COLS), COLS)
        return squares, (wide * gain[:, cols].astype(F32)).astype(BF16), cols

    def whole_part(part, first):
        squares, rows, cols = scaled(part)
        product = jnp.dot(rows, wbuf[cols, :], preferred_element_type=F32)
        total[...] = product if first else total[...] + product
        return squares

    def facts():
        row = lax.broadcasted_iota(jnp.int32, (BLOCK, HD), 0)
        lane = lax.broadcasted_iota(jnp.int32, (BLOCK, HD), 1)
        sign = jnp.where(lane < HD // 2, -1.0, 1.0).astype(F32)
        for half in range(2):
            pos = row + (seq if half == 0 else LAST_BLOCK - seq) * BLOCK
            first = jnp.zeros((BLOCK, HD), jnp.int32)
            bound = LONG
            for j in range(short_lengths.shape[0]):
                first = jnp.where(pos >= bound, bound, first)
                bound = bound + short_lengths[j]
            angles = (pos - first).astype(F32) * fbuf[...]
            cosine[half] = jnp.cos(angles)
            sine[half] = jnp.sin(angles) * sign
            if half == 1:
                first_b[...] = first[:, :1]

    for one in loads[1:5]:
        one.wait()
    squares = whole_part(tp, True)
    for c in range(CHUNKS):
        for way in range(2):
            pass_on(way * CHUNKS + c)
        if c == 0:
            own.wait_recv()
            squares = squares + whole_part(x_hi * 2 + 1 - core, False)
        if c == 1:
            facts()
        if c >= 1:
            for way in range(2):
                share(way * CHUNKS + c - 1)
    for way in range(2):
        share(way * CHUNKS + CHUNKS - 1)
    late = []
    for part in (opposite, (1 - x_hi) * 2 + 1 - core):
        if late:
            for k in range(2 * CHUNKS):
                thirds[k].wait_recv()
        more, rows, cols = scaled(part)
        squares = squares + more
        late.append((rows, cols))
        total[:, :KV_COLS] += jnp.dot(rows, wbuf[cols, :KV_COLS], preferred_element_type=F32)
    factor = lax.rsqrt(squares * (1.0 / D) + norm_eps)

    def turned(half, cols):
        rows = slice(half * BLOCK, (half + 1) * BLOCK)
        u = total[rows, cols] * factor[rows]
        return (u * cosine[half] + pltpu.roll(u, HD // 2, 1) * sine[half]).astype(BF16)

    for half in range(2):
        rows = slice(half * BLOCK, (half + 1) * BLOCK)
        kv[half] = turned(half, slice(0, HD)).reshape(BLOCK // THIRD, THIRD, HD)
        kv[2 + half] = (
            (total[rows, HD:KV_COLS] * factor[rows])
            .astype(BF16)
            .reshape(BLOCK // THIRD, THIRD, HD)
        )

    def chunk(color, off):
        dz, dy, dx = off
        slot = seq_of(
            lax.rem(z + (dz + 8), 8), lax.rem(y + (dy + 4), 4), x_lo if dx == 0 else 1 - x_lo
        )
        return buf.at[:, slot, color]

    def send(color, off, link, src):
        there = shifted(off, link)
        remote(
            src, chunk(color, off), seq_send.at[color],
            seq_recv.at[color, OFFSETS.index(there)], target[link],
        ).start()

    def take(batch):
        for color, off, links in batch:
            here = chunk(color, off)
            remote(
                here, here, seq_send.at[color], seq_recv.at[color, OFFSETS.index(off)], target["x"]
            ).wait_recv()
            for link in links:
                send(color, off, link, here)

    own_copy = pltpu.make_async_copy(kv, buf.at[:, seq], own_sem)
    own_copy.start()
    for color in range(3):
        for link in onward(color, (0, 0, 0), "own"):
            send(color, (0, 0, 0), link, kv.at[:, color])
    for rows, cols in late:
        total[:, KV_COLS:] += jnp.dot(rows, wbuf[cols, KV_COLS:], preferred_element_type=F32)
    for head in range(GROUP):
        for half in range(2):
            q[half, head] = turned(half, slice(KV_COLS + head * HD, KV_COLS + (head + 1) * HD))
    m_ref[...] = jnp.full(m_ref.shape, NEG, F32)
    l_ref[...] = jnp.zeros(l_ref.shape, F32)
    acc_ref[...] = jnp.zeros(acc_ref.shape, F32)
    own_copy.wait()

    def step(half, region, tile, allowed):
        rows = pl.ds(tile * TILE_SLOTS, TILE_SLOTS)
        keys = buf[region, rows].reshape(TILE, HD)
        values = buf[2 + region, rows].reshape(TILE, HD)
        for head in range(GROUP):
            scores = lax.dot_general(
                q[half, head], keys, (((1,), (1,)), ((), ())), preferred_element_type=F32
            )
            if allowed is not None:
                scores = jnp.where(allowed, scores, NEG)
            old = m_ref[half, head]
            new = jnp.maximum(old, jnp.max(scores, axis=1, keepdims=True))
            weights = jnp.exp2(scores * SCALE2 - new * SCALE2)
            if allowed is not None:
                weights = jnp.where(allowed, weights, 0.0)
            keep = jnp.exp2((old - new) * SCALE2)
            m_ref[half, head] = new
            l_ref[half, head] = l_ref[half, head] * keep + jnp.sum(weights, axis=1, keepdims=True)
            acc_ref[half, head] = acc_ref[half, head] * keep + jnp.dot(
                weights.astype(BF16), values, preferred_element_type=F32
            )

    def masked_a(tile):
        row = lax.broadcasted_iota(jnp.int32, (BLOCK, TILE), 0)
        col = lax.broadcasted_iota(jnp.int32, (BLOCK, TILE), 1)
        step(0, 0, tile, col + tile * TILE <= row + seq * BLOCK)

    def masked_b(tile):
        row = lax.broadcasted_iota(jnp.int32, (BLOCK, TILE), 0)
        col = lax.broadcasted_iota(jnp.int32, (BLOCK, TILE), 1)
        slot_in = sum((col >= n * BLOCK).astype(jnp.int32) for n in range(1, TILE_SLOTS))
        key_pos = col - 2 * BLOCK * slot_in + (LAST_BLOCK - tile * TILE_SLOTS) * BLOCK
        row_pos = row + (LAST_BLOCK - seq) * BLOCK
        step(1, 1, tile, (key_pos <= row_pos) & (key_pos >= first_b[...]))

    own_tile = seq // TILE_SLOTS
    in_long = (seq + (LONG_BLOCKS - N_SEQ)) // N_SEQ
    short_end = (seq + 6) // TILE_SLOTS

    def batch_at(unit, part):
        for k in range(N_TILES):
            batch = BATCHES[3 * k + part]
            if batch:
                pl.when(unit == k)(functools.partial(take, batch))

    @pl.loop(0, N_TILES)
    def _(unit):
        rank = unit // 2
        dz = (rank + 1) // 2 * (1 - 2 * ((rank + 1) % 2))
        tile = (z + dz + 8) % 8 * 2 + (y // 2 + unit % 2) % 2
        batch_at(unit, 0)

        @pl.when(in_long == 1)
        def _():
            step(1, 0, tile, None)

        batch_at(unit, 1)

        @pl.when(tile < own_tile)
        def _():
            step(0, 0, tile, None)

        @pl.when(tile == own_tile)
        def _():
            masked_a(tile)

        batch_at(unit, 2)

        @pl.when((in_long == 1) & (tile > own_tile))
        def _():
            step(1, 1, tile, None)

        @pl.when((tile == own_tile) | ((in_long == 0) & (tile > own_tile) & (tile <= short_end)))
        def _():
            masked_b(tile)

    for half in range(2):
        for head in range(GROUP):
            attended[half * BLOCK : (half + 1) * BLOCK, head * HD : (head + 1) * HD] = (
                acc_ref[half, head] / l_ref[half, head]
            ).astype(BF16)

    loads[5].wait()
    far = (1 - x_hi) * 2
    near = x_hi * 2

    def terms(part, way):
        cols = pl.ds(pl.multiple_of(part * COLS, COLS), COLS)
        rows = slice(way * BLOCK, (way + 1) * BLOCK)
        return jnp.dot(attended[rows, :], wout[:, cols], preferred_element_type=F32)

    def to_partner(which, way, part):
        rows = pl.ds(way * BLOCK, BLOCK)
        sendp[which, rows] = terms(part, way).astype(BF16)
        k = 2 * which + way
        return go(
            remote(
                sendp.at[which, rows], recvp.at[which, rows], out_send.at[4 * CHUNKS + k],
                rp.at[k], partner,
            )
        )

    far_copies = [to_partner(0, way, far + 1 - core) for way in range(2)]
    hops = {}
    for way in range(2):
        rows = pl.ds(way * BLOCK, BLOCK)
        mine = terms(far + core, way)
        far_copies[way].wait_recv()
        sendx[rows] = (mine + recvp[0, rows].astype(F32)).astype(BF16)
        for c in range(CHUNKS):
            k = way * CHUNKS + c
            hops[k] = go(
                remote(sendx.at[rows_of(k)], relay_out.at[k], out_send.at[k], o1.at[k], sides[way])
            )
    near_copies = [to_partner(1, way, near + 1 - core) for way in range(2)]
    lands = {}
    for c in range(CHUNKS):
        for way in range(2):
            k = way * CHUNKS + c
            hops[k].wait_recv()
            lands[k] = go(
                remote(
                    relay_out.at[k], recvx.at[rows_of(k)], out_send.at[2 * CHUNKS + k], o2.at[k],
                    sides[way],
                )
            )
    for page in range(ROWS // PAGE):
        ids = lax.broadcasted_iota(jnp.int32, page_slot.shape, 0) * page_slot.shape[
            1
        ] + lax.broadcasted_iota(jnp.int32, page_slot.shape, 1)
        name = jnp.max(jnp.where(page_slot[...] == seq * (ROWS // PAGE) + page, ids, 0))
        block = name // (BLOCK // PAGE)
        part = name - block * (BLOCK // PAGE)
        region = block // N_SEQ
        slot = block + region * (LAST_BLOCK - 2 * block)
        pages[page, 0] = buf[region, slot, part]
        pages[page, 1] = buf[region + 2, slot, part]
    own_x = xbuf[tp].astype(F32)
    for way in range(2):
        rows = slice(way * BLOCK, (way + 1) * BLOCK)
        kept = terms(near + core, way) + own_x[rows]
        near_copies[way].wait_recv()
        kept = kept + recvp[1, rows].astype(F32)
        for c in range(CHUNKS):
            lands[way * CHUNKS + c].wait_recv()
        out[rows, :] = (kept + recvx[rows].astype(F32)).astype(BF16)
    for one in sends:
        one.wait_send()
    for color in range(3):
        sent = buf.at[:, pl.ds(0, N_SEQ - 1), color]
        pltpu.make_async_copy(sent, sent, seq_send.at[color]).wait()


VM = pl.BlockSpec(memory_space=pltpu.VMEM)
SM = pl.BlockSpec(memory_space=pltpu.SMEM)
ANY = pl.BlockSpec(memory_space=pl.ANY)
DMA = pltpu.SemaphoreType.DMA


def local(hidden_in, norm_gain, w_query, w_key, w_value, w_out, short_lengths, page_slot):
    half = np.arange(HD // 2, dtype=np.float32)
    frequency = np.float32(rope_base) ** (-(half * np.float32(2.0)) / np.float32(HD))
    frequency = np.concatenate([frequency, frequency]).astype(np.float32).reshape(1, HD)
    return pl.pallas_call(
        layer_kernel,
        out_shape=(
            jax.ShapeDtypeStruct((ROWS, COLS), BF16),
            jax.ShapeDtypeStruct((ROWS // PAGE, 2, PAGE, HD), BF16),
        ),
        in_specs=[SM, ANY, VM, ANY, VM, ANY, ANY, ANY, ANY],
        out_specs=(VM, VM),
        scratch_shapes=[
            pltpu.VMEM((N_TP, ROWS, COLS), BF16),
            pltpu.VMEM((2 * CHUNKS, CHUNK, COLS), BF16),
            pltpu.VMEM((D, KV_COLS + HEAD_COLS), BF16),
            pltpu.VMEM((HEAD_COLS, D), BF16),
            pltpu.VMEM((1, HD), F32),
            pltpu.VMEM((ROWS, KV_COLS + HEAD_COLS), F32),
            pltpu.VMEM((2, BLOCK, HD), F32),
            pltpu.VMEM((2, BLOCK, HD), F32),
            pltpu.VMEM((BLOCK, 1), jnp.int32),
            pltpu.VMEM((2, GROUP, BLOCK, HD), BF16),
            pltpu.VMEM((4, BLOCK // THIRD, THIRD, HD), BF16),
            pltpu.VMEM((4, N_SEQ, BLOCK // THIRD, THIRD, HD), BF16),
            pltpu.VMEM((2, GROUP, BLOCK, 1), F32),
            pltpu.VMEM((2, GROUP, BLOCK, 1), F32),
            pltpu.VMEM((2, GROUP, BLOCK, HD), F32),
            pltpu.VMEM((ROWS, HEAD_COLS), BF16),
            pltpu.VMEM((2, ROWS, COLS), BF16),
            pltpu.VMEM((2, ROWS, COLS), BF16),
            pltpu.VMEM((ROWS, COLS), BF16),
            pltpu.VMEM((ROWS, COLS), BF16),
            pltpu.VMEM((2 * CHUNKS, CHUNK, COLS), BF16),
            DMA((6,)),
            DMA((6 * CHUNKS + 1,)),
            DMA(()),
            DMA((2 * CHUNKS,)),
            DMA((2 * CHUNKS,)),
            DMA((2 * CHUNKS,)),
            DMA(()),
            DMA((3,)),
            DMA((3, len(OFFSETS))),
            DMA((4 * CHUNKS + 4,)),
            DMA((4,)),
            DMA((2 * CHUNKS,)),
            DMA((2 * CHUNKS,)),
        ],
        compiler_params=pltpu.CompilerParams(
            collective_id=0, has_side_effects=True, vmem_limit_bytes=60 * 1024 * 1024
        ),
        name="layer",
    )(
        short_lengths,
        hidden_in,
        norm_gain.reshape(1, D),
        jnp.asarray(frequency),
        page_slot.reshape(-1, HD),
        w_query,
        w_key,
        w_value,
        w_out,
    )


def solution(mesh):
    placed = (
        P("seq", "tp"),
        P(),
        P(None, "tp"),
        P(None, "tp"),
        P(None, "tp"),
        P("tp", None),
        P(),
        P(),
    )
    return jax.shard_map(
        local,
        mesh=mesh,
        in_specs=placed,
        out_specs=(P("seq", "tp"), P("seq", None, None, "tp")),
        check_vma=False,
    )
```

```python
import functools
import heapq
import math

import jax
import jax.numpy as jnp
import numpy as np
from jax import lax
from jax.experimental import pallas as pl
from jax.experimental.pallas import tpu as pltpu
from jax.sharding import PartitionSpec as P

MESH = pl.DeviceIdType.MESH
F32 = jnp.float32
BF16 = jnp.bfloat16

D = 3072
QH = 12
KVH = 4
HD = 128
PAGE = 64
GROUP = 3
N_SEQ = 64
N_TP = 4
ROWS = 384
BLOCK = 192
COLS = D // N_TP
HEAD_COLS = GROUP * HD
LONG = 16512
LONG_BLOCKS = LONG // BLOCK
THIRD = 64
rope_base = 500000.0
norm_eps = 1e-05
SCALE2 = math.log2(math.e) / math.sqrt(HD)
NEG = -1e30


def onward(color, off, via):
    dz, dy, dx = off
    order = ("xyz", "xzy", "zyx")[color]
    if via == "own":
        links = []
        for axis in order:
            links += ["x"] if axis == "x" else [axis + "+", axis + "-"]
        return links
    links = []
    if via == "z+" and (dz in (-1, -2) or (dz == -3 and (color == 2 or dx == 0))):
        links.append(via)
    if via == "z-" and (dz in (1, 2) or (dz == 3 and color != 2 and dx == 1)):
        links.append(via)
    if via == "y+" and dy == -1 and (dz % 2 == 0 if color == 2 else dx == 0):
        links.append(via)
    if via == "y-" and dy == 1 and (dz % 2 == 1 if color == 2 else dx == 1):
        links.append(via)
    for axis in order[order.index(via[0]) + 1 :]:
        links += ["x"] if axis == "x" else [axis + "+", axis + "-"]
    return links


def shifted(off, link):
    dz, dy, dx = off
    dz += {"z+": -1, "z-": 1}.get(link, 0)
    dy += {"y+": -1, "y-": 1}.get(link, 0)
    dx ^= int(link == "x")
    return (4 if dz == -4 else dz, 2 if dy == -2 else dy, dx)


def plan(copy_us=1.41, hop_us=1.7, step_us=1.3, first_us=1.5):
    free, heap, count, now = {}, [], 0, 0.0

    def issue(color, off, links):
        nonlocal count
        for link in links:
            first = max(now, free.get(link, 0.0))
            free[link] = first + copy_us
            count += 1
            heapq.heappush(
                heap, (first + copy_us + hop_us, count, color, shifted(off, link), link)
            )

    for color in range(3):
        issue(color, (0, 0, 0), onward(color, (0, 0, 0), "own"))
    now = first_us
    missing = [set() for _ in range(STEPS // 3)]
    for unit in range(STEPS // 3):
        dz = plane_of(unit)
        for dy in (0, 1, -1, 2):
            for dx in (0, 1):
                missing[unit] |= {(color, (dz, dy, dx)) for color in range(3)}
        missing[unit] -= {(color, (0, 0, 0)) for color in range(3)}
    taken, batches, batch, step = set(), [], [], 0
    while step < STEPS or heap:
        if heap and heap[0][0] <= now:
            _, _, color, off, link = heapq.heappop(heap)
            links = onward(color, off, link)
            taken.add((color, off))
            batch.append((color, off, links))
            now += 0.03
            issue(color, off, links)
        elif step < STEPS and missing[step // 3] <= taken:
            batches.append(batch)
            batch = []
            step += 1
            now += step_us
        else:
            now = heap[0][0]
    return batches, now


N_PLANES = 8
STEPS = 3 * N_PLANES


def plane_of(rank):
    return (rank + 1) // 2 * (1 - 2 * ((rank + 1) % 2))


BATCHES, _ = plan()
OFFSETS = sorted({off for batch in BATCHES for _, off, _ in batch})


def places():
    seq = lax.axis_index("seq")
    tp = lax.axis_index("tp")
    return seq // 8, (seq // 2) % 4, seq % 2, tp // 2, tp % 2


def seq_of(z, y, x_lo):
    return z * 8 + y * 2 + x_lo


def x_neighbours():
    z, y, x_lo, x_hi, core = places()
    x = x_hi * 2 + x_lo
    ids = []
    for step in (1, 3):
        other = lax.rem(x + step, 4)
        ids.append((seq_of(z, y, other % 2), (other // 2) * 2 + core))
    return x, ids


def greet(ids):
    barrier = pltpu.get_barrier_semaphore()
    for one in ids:
        pl.semaphore_signal(barrier, inc=1, device_id=one, device_id_type=MESH)
    pl.semaphore_wait(barrier, len(ids))


def remote(src, dst, send, recv, target):
    return pltpu.make_async_remote_copy(
        src_ref=src, dst_ref=dst, send_sem=send, recv_sem=recv, device_id=target,
        device_id_type=MESH,
    )


CHUNKS = 6
CHUNK = BLOCK // CHUNKS
SLOTS = N_SEQ // N_PLANES
KEYS = SLOTS * BLOCK
PIECES = 2
PIECE = KEYS // PIECES
QUERIES = GROUP * BLOCK
LAST_BLOCK = 2 * N_SEQ - 1
KV_COLS = 2 * HD


def layer_kernel(
    short_lengths, hidden, gain, frequency, page_slot, wq, wk, wv, w_out, out, pages,
    xbuf, relay, wbuf, wout, fbuf, total, cosine, sine, first_b, q, kv, buf, m_ref, l_ref, acc_ref,
    attended, sendp, recvp, sendx, recvx, relay_out,
    load_sem, send_sem, r0, r1, r2, r3, own_sem, seq_send, seq_recv, out_send, rp, o1, o2,
):
    z, y, x_lo, x_hi, core = places()
    seq = lax.axis_index("seq")
    tp = lax.axis_index("tp")
    loads = [
        pltpu.make_async_copy(hidden, xbuf.at[tp], load_sem.at[0]),
        pltpu.make_async_copy(wk, wbuf.at[:, 0:HD], load_sem.at[1]),
        pltpu.make_async_copy(wv, wbuf.at[:, HD:KV_COLS], load_sem.at[2]),
        pltpu.make_async_copy(wq, wbuf.at[:, KV_COLS:], load_sem.at[3]),
        pltpu.make_async_copy(frequency, fbuf, load_sem.at[4]),
        pltpu.make_async_copy(w_out, wout, load_sem.at[5]),
    ]
    for one in loads:
        one.start()
    x, sides = x_neighbours()
    partner = (seq, x_hi * 2 + 1 - core)
    target = {
        "x": (seq_of(z, y, 1 - x_lo), tp),
        "y+": (seq_of(z, lax.rem(y + 1, 4), x_lo), tp),
        "y-": (seq_of(z, lax.rem(y + 3, 4), x_lo), tp),
        "z+": (seq_of(lax.rem(z + 1, 8), y, x_lo), tp),
        "z-": (seq_of(lax.rem(z + 7, 8), y, x_lo), tp),
    }
    greet([partner] + sides + [target[link] for link in ("y+", "y-", "z+", "z-")])

    sends = []

    def go(copy):
        copy.start()
        sends.append(copy)
        return copy

    def rows_of(k):
        return pl.ds(k * CHUNK, CHUNK)

    opposite = (1 - x_hi) * 2 + core
    loads[0].wait()
    firsts = {}
    for c in range(CHUNKS):
        for way in range(2):
            k = way * CHUNKS + c
            firsts[k] = go(
                remote(xbuf.at[tp, rows_of(k)], relay.at[k], send_sem.at[k], r1.at[k], sides[way])
            )
    own = go(remote(xbuf.at[tp], xbuf.at[tp], send_sem.at[6 * CHUNKS], r0, partner))

    def pass_on(k):
        way = k // CHUNKS
        firsts[k].wait_recv()
        source = lax.rem(x + (3 if way == 0 else 1), 4)
        go(
            remote(
                relay.at[k], xbuf.at[(source // 2) * 2 + core, rows_of(k)],
                send_sem.at[2 * CHUNKS + k], r2.at[k], sides[way],
            )
        )

    thirds = {}

    def share(k):
        here = xbuf.at[opposite, rows_of(k)]
        remote(
            relay.at[k], here, send_sem.at[2 * CHUNKS + k], r2.at[k], sides[k // CHUNKS]
        ).wait_recv()
        thirds[k] = go(remote(here, here, send_sem.at[4 * CHUNKS + k], r3.at[k], partner))

    def scaled(part):
        wide = xbuf[part].astype(F32)
        squares = jnp.sum(wide * wide, axis=1, keepdims=True)
        cols = pl.ds(pl.multiple_of(part * COLS, COLS), COLS)
        return squares, (wide * gain[:, cols].astype(F32)).astype(BF16), cols

    def whole_part(part, first):
        squares, rows, cols = scaled(part)
        product = jnp.dot(rows, wbuf[cols, :], preferred_element_type=F32)
        total[...] = product if first else total[...] + product
        return squares

    def lane_row(shape):
        lane = lax.broadcasted_iota(jnp.int32, shape, 1)
        return lane - BLOCK * sum((lane >= n * BLOCK).astype(jnp.int32) for n in range(1, GROUP))

    def facts():
        row = lax.broadcasted_iota(jnp.int32, (BLOCK, HD), 0)
        lane = lax.broadcasted_iota(jnp.int32, (BLOCK, HD), 1)
        sign = jnp.where(lane < HD // 2, -1.0, 1.0).astype(F32)
        for half in range(2):
            pos = row + (seq if half == 0 else LAST_BLOCK - seq) * BLOCK
            first = jnp.zeros((BLOCK, HD), jnp.int32)
            bound = LONG
            for j in range(short_lengths.shape[0]):
                first = jnp.where(pos >= bound, bound, first)
                bound = bound + short_lengths[j]
            angles = (pos - first).astype(F32) * fbuf[...]
            cosine[half] = jnp.cos(angles)
            sine[half] = jnp.sin(angles) * sign
        pos = lane_row((1, QUERIES)) + (LAST_BLOCK - seq) * BLOCK
        first = jnp.zeros((1, QUERIES), jnp.int32)
        bound = LONG
        for j in range(short_lengths.shape[0]):
            first = jnp.where(pos >= bound, bound, first)
            bound = bound + short_lengths[j]
        first_b[...] = first

    for one in loads[1:5]:
        one.wait()
    squares = whole_part(tp, True)
    for c in range(CHUNKS):
        for way in range(2):
            pass_on(way * CHUNKS + c)
        if c == 0:
            own.wait_recv()
            squares = squares + whole_part(x_hi * 2 + 1 - core, False)
        if c == 1:
            facts()
        if c >= 1:
            for way in range(2):
                share(way * CHUNKS + c - 1)
    for way in range(2):
        share(way * CHUNKS + CHUNKS - 1)
    late = []
    for part in (opposite, (1 - x_hi) * 2 + 1 - core):
        if late:
            for k in range(2 * CHUNKS):
                thirds[k].wait_recv()
        more, rows, cols = scaled(part)
        squares = squares + more
        late.append((rows, cols))
        total[:, :KV_COLS] += jnp.dot(rows, wbuf[cols, :KV_COLS], preferred_element_type=F32)
    factor = lax.rsqrt(squares * (1.0 / D) + norm_eps)

    def turned(half, cols):
        rows = slice(half * BLOCK, (half + 1) * BLOCK)
        u = total[rows, cols] * factor[rows]
        return (u * cosine[half] + pltpu.roll(u, HD // 2, 1) * sine[half]).astype(BF16)

    for half in range(2):
        rows = slice(half * BLOCK, (half + 1) * BLOCK)
        kv[half] = turned(half, slice(0, HD)).reshape(BLOCK // THIRD, THIRD, HD)
        kv[2 + half] = (
            (total[rows, HD:KV_COLS] * factor[rows])
            .astype(BF16)
            .reshape(BLOCK // THIRD, THIRD, HD)
        )

    def chunk(color, off):
        dz, dy, dx = off
        slot = seq_of(
            lax.rem(z + (dz + 8), 8), lax.rem(y + (dy + 4), 4), x_lo if dx == 0 else 1 - x_lo
        )
        return buf.at[:, slot, color]

    def send(color, off, link, src):
        there = shifted(off, link)
        remote(
            src, chunk(color, off), seq_send.at[color],
            seq_recv.at[color, OFFSETS.index(there)], target[link],
        ).start()

    def take(batch):
        for color, off, links in batch:
            here = chunk(color, off)
            remote(
                here, here, seq_send.at[color], seq_recv.at[color, OFFSETS.index(off)], target["x"]
            ).wait_recv()
            for link in links:
                send(color, off, link, here)

    own_copy = pltpu.make_async_copy(kv, buf.at[:, seq], own_sem)
    own_copy.start()
    for color in range(3):
        for link in onward(color, (0, 0, 0), "own"):
            send(color, (0, 0, 0), link, kv.at[:, color])
    for rows, cols in late:
        total[:, KV_COLS:] += jnp.dot(rows, wbuf[cols, KV_COLS:], preferred_element_type=F32)
    for head in range(GROUP):
        for half in range(2):
            q[half, head * BLOCK : (head + 1) * BLOCK] = turned(
                half, slice(KV_COLS + head * HD, KV_COLS + (head + 1) * HD)
            )
    m_ref[...] = jnp.full(m_ref.shape, NEG, F32)
    l_ref[...] = jnp.zeros(l_ref.shape, F32)
    acc_ref[...] = jnp.zeros(acc_ref.shape, F32)
    own_copy.wait()

    def step(half, region, plane, allowed):
        slots = pl.ds(plane * SLOTS, SLOTS)
        keys = buf[region, slots].reshape(KEYS, HD)
        values = buf[2 + region, slots].reshape(KEYS, HD)
        queries = q[half]
        pieces = [slice(n * PIECE, (n + 1) * PIECE) for n in range(PIECES)]
        scores = []
        for n, piece in enumerate(pieces):
            one = lax.dot_general(
                keys[piece], queries, (((1,), (1,)), ((), ())), preferred_element_type=F32
            )
            scores.append(one if allowed is None else jnp.where(allowed(n), one, NEG))
        old = m_ref[half]
        new = old
        for one in scores:
            new = jnp.maximum(new, jnp.max(one, axis=0, keepdims=True))
        shift = new * SCALE2
        keep = jnp.exp2(old * SCALE2 - shift)
        m_ref[half] = new
        denominator = l_ref[half] * keep
        numerator = acc_ref[half] * keep
        for n, piece in enumerate(pieces):
            weights = jnp.exp2(scores[n] * SCALE2 - shift)
            if allowed is not None:
                weights = jnp.where(allowed(n), weights, 0.0)
            denominator = denominator + jnp.sum(weights, axis=0, keepdims=True)
            numerator = numerator + lax.dot_general(
                values[piece], weights.astype(BF16), (((0,), (0,)), ((), ())),
                preferred_element_type=F32,
            )
        l_ref[half] = denominator
        acc_ref[half] = numerator

    def masked_a(plane):
        def allowed(n):
            key = lax.broadcasted_iota(jnp.int32, (PIECE, 1), 0) + (n * PIECE + plane * KEYS)
            return key <= lane_row((1, QUERIES)) + seq * BLOCK

        step(0, 0, plane, allowed)

    def masked_b(plane):
        def allowed(n):
            row = lax.broadcasted_iota(jnp.int32, (PIECE, 1), 0) + n * PIECE
            slot_in = sum((row >= k * BLOCK).astype(jnp.int32) for k in range(1, SLOTS))
            key = row - 2 * BLOCK * slot_in + (LAST_BLOCK - plane * SLOTS) * BLOCK
            query = lane_row((1, QUERIES)) + (LAST_BLOCK - seq) * BLOCK
            return (key <= query) & (key >= first_b[...])

        step(1, 1, plane, allowed)

    in_long = (seq + (LONG_BLOCKS - N_SEQ)) // N_SEQ

    def batch_at(unit, part):
        for k in range(N_PLANES):
            batch = BATCHES[3 * k + part]
            if batch:
                pl.when(unit == k)(functools.partial(take, batch))

    @pl.loop(0, N_PLANES)
    def _(unit):
        dz = (unit + 1) // 2 * (1 - 2 * ((unit + 1) % 2))
        plane = (z + dz + 8) % 8
        batch_at(unit, 0)

        @pl.when(in_long == 1)
        def _():
            step(1, 0, plane, None)

        batch_at(unit, 1)

        @pl.when(plane < z)
        def _():
            step(0, 0, plane, None)

        @pl.when(plane == z)
        def _():
            masked_a(plane)

        batch_at(unit, 2)

        @pl.when((in_long == 1) & (plane > z))
        def _():
            step(1, 1, plane, None)

        @pl.when((plane == z) | ((in_long == 0) & (plane == z + 1)))
        def _():
            masked_b(plane)

    for half in range(2):
        ready = jnp.transpose(acc_ref[half] / l_ref[half]).astype(BF16)
        for head in range(GROUP):
            attended[half * BLOCK : (half + 1) * BLOCK, head * HD : (head + 1) * HD] = ready[
                head * BLOCK : (head + 1) * BLOCK
            ]

    loads[5].wait()
    far = (1 - x_hi) * 2
    near = x_hi * 2

    def terms(part, way):
        cols = pl.ds(pl.multiple_of(part * COLS, COLS), COLS)
        rows = slice(way * BLOCK, (way + 1) * BLOCK)
        return jnp.dot(attended[rows, :], wout[:, cols], preferred_element_type=F32)

    def to_partner(which, way, part):
        rows = pl.ds(way * BLOCK, BLOCK)
        sendp[which, rows] = terms(part, way).astype(BF16)
        k = 2 * which + way
        return go(
            remote(
                sendp.at[which, rows], recvp.at[which, rows], out_send.at[4 * CHUNKS + k],
                rp.at[k], partner,
            )
        )

    far_copies = [to_partner(0, way, far + 1 - core) for way in range(2)]
    hops = {}
    for way in range(2):
        rows = pl.ds(way * BLOCK, BLOCK)
        mine = terms(far + core, way)
        far_copies[way].wait_recv()
        sendx[rows] = (mine + recvp[0, rows].astype(F32)).astype(BF16)
        for c in range(CHUNKS):
            k = way * CHUNKS + c
            hops[k] = go(
                remote(sendx.at[rows_of(k)], relay_out.at[k], out_send.at[k], o1.at[k], sides[way])
            )
    near_copies = [to_partner(1, way, near + 1 - core) for way in range(2)]
    lands = {}
    for c in range(CHUNKS):
        for way in range(2):
            k = way * CHUNKS + c
            hops[k].wait_recv()
            lands[k] = go(
                remote(
                    relay_out.at[k], recvx.at[rows_of(k)], out_send.at[2 * CHUNKS + k], o2.at[k],
                    sides[way],
                )
            )
    for page in range(ROWS // PAGE):
        ids = lax.broadcasted_iota(jnp.int32, page_slot.shape, 0) * page_slot.shape[
            1
        ] + lax.broadcasted_iota(jnp.int32, page_slot.shape, 1)
        name = jnp.max(jnp.where(page_slot[...] == seq * (ROWS // PAGE) + page, ids, 0))
        block = name // (BLOCK // PAGE)
        part = name - block * (BLOCK // PAGE)
        region = block // N_SEQ
        slot = block + region * (LAST_BLOCK - 2 * block)
        pages[page, 0] = buf[region, slot, part]
        pages[page, 1] = buf[region + 2, slot, part]
    own_x = xbuf[tp].astype(F32)
    for way in range(2):
        rows = slice(way * BLOCK, (way + 1) * BLOCK)
        kept = terms(near + core, way) + own_x[rows]
        near_copies[way].wait_recv()
        kept = kept + recvp[1, rows].astype(F32)
        for c in range(CHUNKS):
            lands[way * CHUNKS + c].wait_recv()
        out[rows, :] = (kept + recvx[rows].astype(F32)).astype(BF16)
    for one in sends:
        one.wait_send()
    for color in range(3):
        sent = buf.at[:, pl.ds(0, N_SEQ - 1), color]
        pltpu.make_async_copy(sent, sent, seq_send.at[color]).wait()


VM = pl.BlockSpec(memory_space=pltpu.VMEM)
SM = pl.BlockSpec(memory_space=pltpu.SMEM)
ANY = pl.BlockSpec(memory_space=pl.ANY)
DMA = pltpu.SemaphoreType.DMA


def local(hidden_in, norm_gain, w_query, w_key, w_value, w_out, short_lengths, page_slot):
    half = np.arange(HD // 2, dtype=np.float32)
    frequency = np.float32(rope_base) ** (-(half * np.float32(2.0)) / np.float32(HD))
    frequency = np.concatenate([frequency, frequency]).astype(np.float32).reshape(1, HD)
    return pl.pallas_call(
        layer_kernel,
        out_shape=(
            jax.ShapeDtypeStruct((ROWS, COLS), BF16),
            jax.ShapeDtypeStruct((ROWS // PAGE, 2, PAGE, HD), BF16),
        ),
        in_specs=[SM, ANY, VM, ANY, VM, ANY, ANY, ANY, ANY],
        out_specs=(VM, VM),
        scratch_shapes=[
            pltpu.VMEM((N_TP, ROWS, COLS), BF16),
            pltpu.VMEM((2 * CHUNKS, CHUNK, COLS), BF16),
            pltpu.VMEM((D, KV_COLS + HEAD_COLS), BF16),
            pltpu.VMEM((HEAD_COLS, D), BF16),
            pltpu.VMEM((1, HD), F32),
            pltpu.VMEM((ROWS, KV_COLS + HEAD_COLS), F32),
            pltpu.VMEM((2, BLOCK, HD), F32),
            pltpu.VMEM((2, BLOCK, HD), F32),
            pltpu.VMEM((1, QUERIES), jnp.int32),
            pltpu.VMEM((2, QUERIES, HD), BF16),
            pltpu.VMEM((4, BLOCK // THIRD, THIRD, HD), BF16),
            pltpu.VMEM((4, N_SEQ, BLOCK // THIRD, THIRD, HD), BF16),
            pltpu.VMEM((2, 1, QUERIES), F32),
            pltpu.VMEM((2, 1, QUERIES), F32),
            pltpu.VMEM((2, HD, QUERIES), F32),
            pltpu.VMEM((ROWS, HEAD_COLS), BF16),
            pltpu.VMEM((2, ROWS, COLS), BF16),
            pltpu.VMEM((2, ROWS, COLS), BF16),
            pltpu.VMEM((ROWS, COLS), BF16),
            pltpu.VMEM((ROWS, COLS), BF16),
            pltpu.VMEM((2 * CHUNKS, CHUNK, COLS), BF16),
            DMA((6,)),
            DMA((6 * CHUNKS + 1,)),
            DMA(()),
            DMA((2 * CHUNKS,)),
            DMA((2 * CHUNKS,)),
            DMA((2 * CHUNKS,)),
            DMA(()),
            DMA((3,)),
            DMA((3, len(OFFSETS))),
            DMA((4 * CHUNKS + 4,)),
            DMA((4,)),
            DMA((2 * CHUNKS,)),
            DMA((2 * CHUNKS,)),
        ],
        compiler_params=pltpu.CompilerParams(
            collective_id=0, has_side_effects=True, vmem_limit_bytes=60 * 1024 * 1024
        ),
        name="layer",
    )(
        short_lengths,
        hidden_in,
        norm_gain.reshape(1, D),
        jnp.asarray(frequency),
        page_slot.reshape(-1, HD),
        w_query,
        w_key,
        w_value,
        w_out,
    )


def solution(mesh):
    placed = (
        P("seq", "tp"),
        P(),
        P(None, "tp"),
        P(None, "tp"),
        P(None, "tp"),
        P("tp", None),
        P(),
        P(),
    )
    return jax.shard_map(
        local,
        mesh=mesh,
        in_specs=placed,
        out_specs=(P("seq", "tp"), P("seq", None, None, "tp")),
        check_vma=False,
    )
```

```python
import functools
import heapq
import math

import jax
import jax.numpy as jnp
import numpy as np
from jax import lax
from jax.experimental import pallas as pl
from jax.experimental.pallas import tpu as pltpu
from jax.sharding import PartitionSpec as P

MESH = pl.DeviceIdType.MESH
F32 = jnp.float32
BF16 = jnp.bfloat16

D = 3072
QH = 12
KVH = 4
HD = 128
PAGE = 64
GROUP = 3
N_SEQ = 64
N_TP = 4
ROWS = 384
BLOCK = 192
COLS = D // N_TP
HEAD_COLS = GROUP * HD
LONG = 16512
LONG_BLOCKS = LONG // BLOCK
THIRD = 64
rope_base = 500000.0
norm_eps = 1e-05
SCALE2 = math.log2(math.e) / math.sqrt(HD)
NEG = -1e30


def onward(color, off, via):
    dz, dy, dx = off
    order = ("xyz", "xzy", "zyx")[color]
    if via == "own":
        links = []
        for axis in order:
            links += ["x"] if axis == "x" else [axis + "+", axis + "-"]
        return links
    links = []
    if via == "z+" and (dz in (-1, -2) or (dz == -3 and (color == 2 or dx == 0))):
        links.append(via)
    if via == "z-" and (dz in (1, 2) or (dz == 3 and color != 2 and dx == 1)):
        links.append(via)
    if via == "y+" and dy == -1 and (dz % 2 == 0 if color == 2 else dx == 0):
        links.append(via)
    if via == "y-" and dy == 1 and (dz % 2 == 1 if color == 2 else dx == 1):
        links.append(via)
    for axis in order[order.index(via[0]) + 1 :]:
        links += ["x"] if axis == "x" else [axis + "+", axis + "-"]
    return links


def shifted(off, link):
    dz, dy, dx = off
    dz += {"z+": -1, "z-": 1}.get(link, 0)
    dy += {"y+": -1, "y-": 1}.get(link, 0)
    dx ^= int(link == "x")
    return (4 if dz == -4 else dz, 2 if dy == -2 else dy, dx)


N_PLANES = 8
STEPS = 3 * N_PLANES
STARTS = (2, 0, 1)
START_US = (0.0, 4.2, 6.3)
CUTS = (0.5, 3.2, 4.7, 5.0, 6.8)


def plane_of(rank):
    return (rank + 1) // 2 * (1 - 2 * ((rank + 1) % 2))


def timetable(copy_us=1.41, hop_us=1.7, ahead_us=4.0):
    heap, count, queues, busy, arrived, served = [], 0, {}, {}, {}, []

    def put(now, what):
        nonlocal count
        count += 1
        heapq.heappush(heap, (now, count, what))

    def kick(link, now):
        if busy.get(link, 0.0) > now + 1e-6 or not queues.get(link):
            return
        _, _, color, off = heapq.heappop(queues[link])
        busy[link] = now + copy_us
        served.append((now, color, off, link))
        put(now + copy_us, (link,))
        put(now + copy_us + hop_us, (color, shifted(off, link), link))

    for color, start in zip(STARTS, START_US):
        put(start, (color, (0, 0, 0), "own"))
    while heap:
        now, order, what = heapq.heappop(heap)
        if len(what) == 1:
            kick(what[0], now)
            continue
        color, off, via = what
        arrived[color, off] = now
        for link in onward(color, off, via):
            count += 1
            heapq.heappush(queues.setdefault(link, []), (abs(off[0]), count, color, off))
            kick(link, now)
    actions = [(now, 0, one, None) for one, now in arrived.items() if one[1] != (0, 0, 0)]
    last = {}
    for start, color, off, link in served:
        due = max(arrived[color, off], start - ahead_us, last.get(link, 0.0))
        last[link] = due
        actions.append((due, 1, (color, off), link))
    actions.sort(key=lambda one: one[:2])
    return actions


def plan(step_us=1.2, first_us=1.5):
    actions = timetable()
    early = []
    for cut in CUTS:
        early.append([one for one in actions if one[0] <= cut])
        actions = actions[len(early[-1]) :]
    missing = []
    for unit in range(N_PLANES):
        dz = plane_of(unit)
        missing.append(
            {
                (color, (dz, dy, dx))
                for color in range(3)
                for dy in (0, 1, -1, 2)
                for dx in (0, 1)
                if (dz, dy, dx) != (0, 0, 0)
            }
        )
    taken = {one[2] for batch in early for one in batch if one[1] == 0}
    now, step, batches, batch = CUTS[-1] + first_us, 0, [], []
    while step < STEPS or actions:
        if actions and (actions[0][0] <= now or step == STEPS):
            one = actions.pop(0)
            if one[1] == 0:
                taken.add(one[2])
            now = max(now, one[0]) + 0.02
            batch.append(one)
        elif step < STEPS and missing[step // 3] <= taken:
            batches.append(batch)
            batch = []
            step += 1
            now += step_us
        else:
            now = actions[0][0]
    assert not batch
    return early, batches, now


EARLY, BATCHES, _ = plan()
OFFSETS = sorted({one[2][1] for batch in EARLY + BATCHES for one in batch if one[1] == 0})


def places():
    seq = lax.axis_index("seq")
    tp = lax.axis_index("tp")
    return seq // 8, (seq // 2) % 4, seq % 2, tp // 2, tp % 2


def seq_of(z, y, x_lo):
    return z * 8 + y * 2 + x_lo


def x_neighbours():
    z, y, x_lo, x_hi, core = places()
    x = x_hi * 2 + x_lo
    ids = []
    for step in (1, 3):
        other = lax.rem(x + step, 4)
        ids.append((seq_of(z, y, other % 2), (other // 2) * 2 + core))
    return x, ids


def greet(ids):
    barrier = pltpu.get_barrier_semaphore()
    for one in ids:
        pl.semaphore_signal(barrier, inc=1, device_id=one, device_id_type=MESH)
    pl.semaphore_wait(barrier, len(ids))


def remote(src, dst, send, recv, target):
    return pltpu.make_async_remote_copy(
        src_ref=src, dst_ref=dst, send_sem=send, recv_sem=recv, device_id=target,
        device_id_type=MESH,
    )


CHUNKS = 6
CHUNK = BLOCK // CHUNKS
SLOTS = N_SEQ // N_PLANES
KEYS = SLOTS * BLOCK
PIECES = 2
PIECE = KEYS // PIECES
QUERIES = GROUP * BLOCK
LAST_BLOCK = 2 * N_SEQ - 1
KV_COLS = 2 * HD


def layer_kernel(
    short_lengths, hidden, gain, frequency, page_slot, wq, wk, wv, w_out, out, pages,
    xbuf, relay, wbuf, wout, fbuf, total, cosine, sine, first_b, q, kv, buf, m_ref, l_ref, acc_ref,
    attended, sendp, recvp, sendx, recvx, relay_out,
    load_sem, send_sem, r0, r1, r2, r3, own_sem, seq_send, seq_recv, out_send, rp, o1, o2,
):
    z, y, x_lo, x_hi, core = places()
    seq = lax.axis_index("seq")
    tp = lax.axis_index("tp")
    loads = [
        pltpu.make_async_copy(hidden, xbuf.at[tp], load_sem.at[0]),
        pltpu.make_async_copy(wk, wbuf.at[:, 0:HD], load_sem.at[1]),
        pltpu.make_async_copy(wv, wbuf.at[:, HD:KV_COLS], load_sem.at[2]),
        pltpu.make_async_copy(wq, wbuf.at[:, KV_COLS:], load_sem.at[3]),
        pltpu.make_async_copy(frequency, fbuf, load_sem.at[4]),
        pltpu.make_async_copy(w_out, wout, load_sem.at[5]),
    ]
    for one in loads:
        one.start()
    x, sides = x_neighbours()
    partner = (seq, x_hi * 2 + 1 - core)
    target = {
        "x": (seq_of(z, y, 1 - x_lo), tp),
        "y+": (seq_of(z, lax.rem(y + 1, 4), x_lo), tp),
        "y-": (seq_of(z, lax.rem(y + 3, 4), x_lo), tp),
        "z+": (seq_of(lax.rem(z + 1, 8), y, x_lo), tp),
        "z-": (seq_of(lax.rem(z + 7, 8), y, x_lo), tp),
    }
    greet([partner] + sides + [target[link] for link in ("y+", "y-", "z+", "z-")])

    sends = []

    def go(copy):
        copy.start()
        sends.append(copy)
        return copy

    def rows_of(k):
        return pl.ds(k * CHUNK, CHUNK)

    def in_start_order(c):
        return STARTS[c // 2] * 2 + c % 2

    opposite = (1 - x_hi) * 2 + core
    loads[0].wait()
    firsts = {}

    def start_own(c):
        for way in range(2):
            k = way * CHUNKS + in_start_order(c)
            firsts[k] = go(
                remote(xbuf.at[tp, rows_of(k)], relay.at[k], send_sem.at[k], r1.at[k], sides[way])
            )

    for c in range(3):
        start_own(c)
    own = go(remote(xbuf.at[tp], xbuf.at[tp], send_sem.at[6 * CHUNKS], r0, partner))

    def pass_on(k):
        way = k // CHUNKS
        firsts[k].wait_recv()
        source = lax.rem(x + (3 if way == 0 else 1), 4)
        go(
            remote(
                relay.at[k], xbuf.at[(source // 2) * 2 + core, rows_of(k)],
                send_sem.at[2 * CHUNKS + k], r2.at[k], sides[way],
            )
        )

    thirds = {}

    def share(k):
        here = xbuf.at[opposite, rows_of(k)]
        remote(
            relay.at[k], here, send_sem.at[2 * CHUNKS + k], r2.at[k], sides[k // CHUNKS]
        ).wait_recv()
        thirds[k] = go(remote(here, here, send_sem.at[4 * CHUNKS + k], r3.at[k], partner))

    def weighted(wide, part):
        cols = pl.ds(pl.multiple_of(part * COLS, COLS), COLS)
        return (wide * gain[cols].astype(F32)[None, :]).astype(BF16), cols

    def whole_part(part, first):
        wide = xbuf[part].astype(F32)
        squares = jnp.sum(wide * wide, axis=1, keepdims=True)
        rows, cols = weighted(wide, part)
        product = jnp.dot(rows, wbuf[cols, :], preferred_element_type=F32)
        total[...] = product if first else total[...] + product
        return squares

    def lane_row(shape):
        lane = lax.broadcasted_iota(jnp.int32, shape, 1)
        return lane - BLOCK * sum((lane >= n * BLOCK).astype(jnp.int32) for n in range(1, GROUP))

    def facts():
        row = lax.broadcasted_iota(jnp.int32, (BLOCK, HD), 0)
        lane = lax.broadcasted_iota(jnp.int32, (BLOCK, HD), 1)
        sign = jnp.where(lane < HD // 2, -1.0, 1.0).astype(F32)
        for half in range(2):
            pos = row + (seq if half == 0 else LAST_BLOCK - seq) * BLOCK
            first = jnp.zeros((BLOCK, HD), jnp.int32)
            bound = LONG
            for j in range(short_lengths.shape[0]):
                first = jnp.where(pos >= bound, bound, first)
                bound = bound + short_lengths[j]
            angles = (pos - first).astype(F32) * fbuf[...]
            cosine[half] = jnp.cos(angles)
            sine[half] = jnp.sin(angles) * sign
        pos = lane_row((1, QUERIES)) + (LAST_BLOCK - seq) * BLOCK
        first = jnp.zeros((1, QUERIES), jnp.int32)
        bound = LONG
        for j in range(short_lengths.shape[0]):
            first = jnp.where(pos >= bound, bound, first)
            bound = bound + short_lengths[j]
        first_b[...] = first

    def chunk(color, off):
        dz, dy, dx = off
        slot = seq_of(
            lax.rem(z + (dz + 8), 8), lax.rem(y + (dy + 4), 4), x_lo if dx == 0 else 1 - x_lo
        )
        return buf.at[:, slot, color]

    def send(color, off, link, src):
        there = shifted(off, link)
        remote(
            src, chunk(color, off), seq_send.at[color],
            seq_recv.at[color, OFFSETS.index(there)], target[link],
        ).start()

    def take(batch):
        for _, sends_it, (color, off), link in batch:
            here = chunk(color, off)
            if not sends_it:
                remote(
                    here, here, seq_send.at[color], seq_recv.at[color, OFFSETS.index(off)],
                    target["x"],
                ).wait_recv()
            elif off == (0, 0, 0):
                send(color, off, link, kv.at[:, color])
            else:
                send(color, off, link, here)

    def own_copy(color):
        return pltpu.make_async_copy(kv.at[:, color], buf.at[:, seq, color], own_sem.at[color])

    far_parts = (opposite, (1 - x_hi) * 2 + 1 - core)

    def third(color):
        spans = [slice(half * BLOCK + color * THIRD, half * BLOCK + (color + 1) * THIRD)
                 for half in range(2)]
        for k in (2 * color, 2 * color + 1):
            for way in range(2):
                thirds[way * CHUNKS + k].wait_recv()
        sums = jnp.concatenate([squares[span] for span in spans])
        product = jnp.concatenate([total[span, :KV_COLS] for span in spans])
        kept = []
        for part in far_parts:
            wide = jnp.concatenate([xbuf[part, span] for span in spans]).astype(F32)
            sums = sums + jnp.sum(wide * wide, axis=1, keepdims=True)
            rows, cols = weighted(wide, part)
            kept.append(rows)
            product = product + jnp.dot(
                rows, wbuf[cols, :KV_COLS], preferred_element_type=F32
            )
        factor = lax.rsqrt(sums * (1.0 / D) + norm_eps)
        product = product * factor
        u = product[:, :HD]
        turned_u = pltpu.roll(u, HD // 2, 1)
        for half in range(2):
            rows = slice(half * THIRD, (half + 1) * THIRD)
            angle = slice(color * THIRD, (color + 1) * THIRD)
            kv[half, color] = (
                u[rows] * cosine[half, angle] + turned_u[rows] * sine[half, angle]
            ).astype(BF16)
            kv[2 + half, color] = product[rows, HD:].astype(BF16)
        own_copy(color).start()
        return kept, factor

    for one in loads[1:5]:
        one.wait()
    squares = whole_part(tp, True)
    late = []
    def both(do, c):
        for way in range(2):
            do(way * CHUNKS + in_start_order(c))

    both(pass_on, 0)
    start_own(3)
    own.wait_recv()
    squares = squares + whole_part(x_hi * 2 + 1 - core, False)
    both(pass_on, 1)
    start_own(4)
    both(pass_on, 2)
    start_own(5)
    facts()
    both(share, 0)
    both(pass_on, 3)
    both(share, 1)
    both(pass_on, 4)
    late.append(third(STARTS[0]))
    take(EARLY[0])
    both(share, 2)
    both(pass_on, 5)
    both(share, 3)
    both(share, 4)
    take(EARLY[1])
    late.append(third(STARTS[1]))
    take(EARLY[2])
    both(share, 5)
    take(EARLY[3])
    late.append(third(STARTS[2]))
    take(EARLY[4])
    for n, part in enumerate(far_parts):
        cols = pl.ds(pl.multiple_of(part * COLS, COLS), COLS)
        product = jnp.dot(
            jnp.concatenate([kept[n] for kept, _ in late]), wbuf[cols, KV_COLS:],
            preferred_element_type=F32,
        )
        for at, color in enumerate(STARTS):
            for half in range(2):
                first = half * BLOCK + color * THIRD
                there = (2 * at + half) * THIRD
                total[first : first + THIRD, KV_COLS:] += product[there : there + THIRD]
    for half in range(2):
        factor = jnp.concatenate(
            [late[STARTS.index(color)][1][half * THIRD : (half + 1) * THIRD] for color in range(3)]
        )
        for head in range(GROUP):
            u = total[
                half * BLOCK : (half + 1) * BLOCK,
                KV_COLS + head * HD : KV_COLS + (head + 1) * HD,
            ] * factor
            q[half, head * BLOCK : (head + 1) * BLOCK] = (
                u * cosine[half] + pltpu.roll(u, HD // 2, 1) * sine[half]
            ).astype(BF16)
    m_ref[...] = jnp.full(m_ref.shape, NEG, F32)
    l_ref[...] = jnp.zeros(l_ref.shape, F32)
    acc_ref[...] = jnp.zeros(acc_ref.shape, F32)
    for color in range(3):
        own_copy(color).wait()

    def step(half, region, plane, allowed):
        slots = pl.ds(plane * SLOTS, SLOTS)
        keys = buf[region, slots].reshape(KEYS, HD)
        values = buf[2 + region, slots].reshape(KEYS, HD)
        queries = q[half]
        pieces = [slice(n * PIECE, (n + 1) * PIECE) for n in range(PIECES)]
        scores = []
        for n, piece in enumerate(pieces):
            one = lax.dot_general(
                keys[piece], queries, (((1,), (1,)), ((), ())), preferred_element_type=F32
            )
            scores.append(one if allowed is None else jnp.where(allowed(n), one, NEG))
        old = m_ref[half]
        new = old
        for one in scores:
            new = jnp.maximum(new, jnp.max(one, axis=0, keepdims=True))
        shift = new * SCALE2
        keep = jnp.exp2(old * SCALE2 - shift)
        m_ref[half] = new
        denominator = l_ref[half] * keep
        numerator = acc_ref[half] * keep
        for n, piece in enumerate(pieces):
            weights = jnp.exp2(scores[n] * SCALE2 - shift)
            if allowed is not None:
                weights = jnp.where(allowed(n), weights, 0.0)
            denominator = denominator + jnp.sum(weights, axis=0, keepdims=True)
            numerator = numerator + lax.dot_general(
                values[piece], weights.astype(BF16), (((0,), (0,)), ((), ())),
                preferred_element_type=F32,
            )
        l_ref[half] = denominator
        acc_ref[half] = numerator

    def masked_a(plane):
        def allowed(n):
            key = lax.broadcasted_iota(jnp.int32, (PIECE, 1), 0) + (n * PIECE + plane * KEYS)
            return key <= lane_row((1, QUERIES)) + seq * BLOCK

        step(0, 0, plane, allowed)

    def masked_b(plane):
        def allowed(n):
            row = lax.broadcasted_iota(jnp.int32, (PIECE, 1), 0) + n * PIECE
            slot_in = sum((row >= k * BLOCK).astype(jnp.int32) for k in range(1, SLOTS))
            key = row - 2 * BLOCK * slot_in + (LAST_BLOCK - plane * SLOTS) * BLOCK
            query = lane_row((1, QUERIES)) + (LAST_BLOCK - seq) * BLOCK
            return (key <= query) & (key >= first_b[...])

        step(1, 1, plane, allowed)

    in_long = (seq + (LONG_BLOCKS - N_SEQ)) // N_SEQ

    def batch_at(unit, part):
        for k in range(N_PLANES):
            batch = BATCHES[3 * k + part]
            if batch:
                pl.when(unit == k)(functools.partial(take, batch))

    def finish(half):
        ready = jnp.transpose(acc_ref[half] / l_ref[half]).astype(BF16)
        for head in range(GROUP):
            attended[half * BLOCK : (half + 1) * BLOCK, head * HD : (head + 1) * HD] = ready[
                head * BLOCK : (head + 1) * BLOCK
            ]

    far = (1 - x_hi) * 2
    near = x_hi * 2

    def terms(part, half):
        cols = pl.ds(pl.multiple_of(part * COLS, COLS), COLS)
        return jnp.dot(
            attended[half * BLOCK : (half + 1) * BLOCK, :], wout[:, cols],
            preferred_element_type=F32,
        )

    def partner_copy(which, half):
        rows = pl.ds(half * BLOCK, BLOCK)
        k = 2 * which + half
        return remote(
            sendp.at[which, rows], recvp.at[which, rows], out_send.at[4 * CHUNKS + k], rp.at[k],
            partner,
        )

    def to_partner(which, half, part):
        sendp[which, pl.ds(half * BLOCK, BLOCK)] = terms(part, half).astype(BF16)
        partner_copy(which, half).start()

    def hop(k):
        return remote(
            sendx.at[rows_of(k)], relay_out.at[k], out_send.at[k], o1.at[k], sides[k % 2]
        )

    def land(k):
        return remote(
            relay_out.at[k], recvx.at[rows_of(k)], out_send.at[2 * CHUNKS + k], o2.at[k],
            sides[k % 2],
        )

    def chunks_of(half):
        return range(half * CHUNKS, (half + 1) * CHUNKS)

    def cross(half, mine):
        rows = pl.ds(half * BLOCK, BLOCK)
        partner_copy(0, half).wait_recv()
        sendx[rows] = (mine + recvp[0, rows].astype(F32)).astype(BF16)
        for k in chunks_of(half):
            hop(k).start()

    loads[5].wait()

    @pl.loop(0, N_PLANES)
    def _(unit):
        dz = (unit + 1) // 2 * (1 - 2 * ((unit + 1) % 2))
        plane = (z + dz + 8) % 8
        batch_at(unit, 0)

        @pl.when(plane < z)
        def _():
            step(0, 0, plane, None)

        @pl.when(plane == z)
        def _():
            masked_a(plane)

        @pl.when(unit == N_PLANES - 1)
        def _():
            finish(0)
            to_partner(0, 0, far + 1 - core)

        batch_at(unit, 1)

        @pl.when(in_long == 1)
        def _():
            step(1, 0, plane, None)

        @pl.when(unit == N_PLANES - 1)
        def _():
            cross(0, terms(far + core, 0))

        batch_at(unit, 2)

        @pl.when((in_long == 1) & (plane > z))
        def _():
            step(1, 1, plane, None)

        @pl.when((plane == z) | ((in_long == 0) & (plane == z + 1)))
        def _():
            masked_b(plane)

    finish(1)
    to_partner(0, 1, far + 1 - core)
    mine = terms(far + core, 1)
    for half in range(2):
        to_partner(1, half, near + 1 - core)
    cross(1, mine)
    for k in chunks_of(0):
        hop(k).wait_recv()
        land(k).start()
    for page in range(ROWS // PAGE):
        ids = lax.broadcasted_iota(jnp.int32, page_slot.shape, 0) * page_slot.shape[
            1
        ] + lax.broadcasted_iota(jnp.int32, page_slot.shape, 1)
        name = jnp.max(jnp.where(page_slot[...] == seq * (ROWS // PAGE) + page, ids, 0))
        block = name // (BLOCK // PAGE)
        part = name - block * (BLOCK // PAGE)
        region = block // N_SEQ
        slot = block + region * (LAST_BLOCK - 2 * block)
        pages[page, 0] = buf[region, slot, part]
        pages[page, 1] = buf[region + 2, slot, part]
    for k in chunks_of(1):
        hop(k).wait_recv()
        land(k).start()
    own_x = xbuf[tp].astype(F32)
    for half in range(2):
        rows = slice(half * BLOCK, (half + 1) * BLOCK)
        kept = terms(near + core, half) + own_x[rows]
        partner_copy(1, half).wait_recv()
        kept = kept + recvp[1, rows].astype(F32)
        for k in chunks_of(half):
            land(k).wait_recv()
        out[rows, :] = (kept + recvx[rows].astype(F32)).astype(BF16)
    for one in sends:
        one.wait_send()
    for half in range(2):
        for which in range(2):
            partner_copy(which, half).wait_send()
        for k in chunks_of(half):
            hop(k).wait_send()
            land(k).wait_send()
    for color in range(3):
        sent = buf.at[:, pl.ds(0, N_SEQ - 1), color]
        pltpu.make_async_copy(sent, sent, seq_send.at[color]).wait()


VM = pl.BlockSpec(memory_space=pltpu.VMEM)
SM = pl.BlockSpec(memory_space=pltpu.SMEM)
ANY = pl.BlockSpec(memory_space=pl.ANY)
DMA = pltpu.SemaphoreType.DMA


def in_hbm(one):
    return pltpu.with_memory_space_constraint(one, pltpu.HBM)


def local(hidden_in, norm_gain, w_query, w_key, w_value, w_out, short_lengths, page_slot):
    half = np.arange(HD // 2, dtype=np.float32)
    frequency = np.float32(rope_base) ** (-(half * np.float32(2.0)) / np.float32(HD))
    frequency = np.concatenate([frequency, frequency]).astype(np.float32).reshape(1, HD)
    return pl.pallas_call(
        layer_kernel,
        out_shape=(
            jax.ShapeDtypeStruct((ROWS, COLS), BF16),
            jax.ShapeDtypeStruct((ROWS // PAGE, 2, PAGE, HD), BF16),
        ),
        in_specs=[SM, ANY, VM, ANY, VM, ANY, ANY, ANY, ANY],
        out_specs=(VM, VM),
        scratch_shapes=[
            pltpu.VMEM((N_TP, ROWS, COLS), BF16),
            pltpu.VMEM((2 * CHUNKS, CHUNK, COLS), BF16),
            pltpu.VMEM((D, KV_COLS + HEAD_COLS), BF16),
            pltpu.VMEM((HEAD_COLS, D), BF16),
            pltpu.VMEM((1, HD), F32),
            pltpu.VMEM((ROWS, KV_COLS + HEAD_COLS), F32),
            pltpu.VMEM((2, BLOCK, HD), F32),
            pltpu.VMEM((2, BLOCK, HD), F32),
            pltpu.VMEM((1, QUERIES), jnp.int32),
            pltpu.VMEM((2, QUERIES, HD), BF16),
            pltpu.VMEM((4, BLOCK // THIRD, THIRD, HD), BF16),
            pltpu.VMEM((4, N_SEQ, BLOCK // THIRD, THIRD, HD), BF16),
            pltpu.VMEM((2, 1, QUERIES), F32),
            pltpu.VMEM((2, 1, QUERIES), F32),
            pltpu.VMEM((2, HD, QUERIES), F32),
            pltpu.VMEM((ROWS, HEAD_COLS), BF16),
            pltpu.VMEM((2, ROWS, COLS), BF16),
            pltpu.VMEM((2, ROWS, COLS), BF16),
            pltpu.VMEM((ROWS, COLS), BF16),
            pltpu.VMEM((ROWS, COLS), BF16),
            pltpu.VMEM((2 * CHUNKS, CHUNK, COLS), BF16),
            DMA((6,)),
            DMA((6 * CHUNKS + 1,)),
            DMA(()),
            DMA((2 * CHUNKS,)),
            DMA((2 * CHUNKS,)),
            DMA((2 * CHUNKS,)),
            DMA((3,)),
            DMA((3,)),
            DMA((3, len(OFFSETS))),
            DMA((4 * CHUNKS + 4,)),
            DMA((4,)),
            DMA((2 * CHUNKS,)),
            DMA((2 * CHUNKS,)),
        ],
        compiler_params=pltpu.CompilerParams(
            collective_id=0, has_side_effects=True, vmem_limit_bytes=44 * 1024 * 1024
        ),
        name="layer",
    )(*(in_hbm(one) for one in (
        short_lengths,
        hidden_in,
        norm_gain,
        jnp.asarray(frequency),
        page_slot.reshape(-1, HD),
        w_query,
        w_key,
        w_value,
        w_out,
    )))


def solution(mesh):
    placed = (
        P("seq", "tp"),
        P(),
        P(None, "tp"),
        P(None, "tp"),
        P(None, "tp"),
        P("tp", None),
        P(),
        P(),
    )
    return jax.shard_map(
        local,
        mesh=mesh,
        in_specs=placed,
        out_specs=(P("seq", "tp"), P("seq", None, None, "tp")),
        check_vma=False,
    )
```

```python
import functools
import heapq
import math

import jax
import jax.numpy as jnp
import numpy as np
from jax import lax
from jax.experimental import pallas as pl
from jax.experimental.pallas import tpu as pltpu
from jax.sharding import PartitionSpec as P

MESH = pl.DeviceIdType.MESH
F32 = jnp.float32
BF16 = jnp.bfloat16

D = 3072
QH = 12
KVH = 4
HD = 128
PAGE = 64
GROUP = 3
N_SEQ = 64
N_TP = 4
ROWS = 384
BLOCK = 192
COLS = D // N_TP
HEAD_COLS = GROUP * HD
LONG = 16512
LONG_BLOCKS = LONG // BLOCK
THIRD = 64
rope_base = 500000.0
norm_eps = 1e-05
SCALE2 = math.log2(math.e) / math.sqrt(HD)
NEG = -1e30


def onward(color, off, via):
    dz, dy, dx = off
    order = ("xyz", "xzy", "zyx")[color]
    if via == "own":
        links = []
        for axis in order:
            links += ["x"] if axis == "x" else [axis + "+", axis + "-"]
        return links
    links = []
    if via == "z+" and (dz in (-1, -2) or (dz == -3 and (color == 2 or dx == 0))):
        links.append(via)
    if via == "z-" and (dz in (1, 2) or (dz == 3 and color != 2 and dx == 1)):
        links.append(via)
    if via == "y+" and dy == -1 and (dz % 2 == 0 if color == 2 else dx == 0):
        links.append(via)
    if via == "y-" and dy == 1 and (dz % 2 == 1 if color == 2 else dx == 1):
        links.append(via)
    for axis in order[order.index(via[0]) + 1 :]:
        links += ["x"] if axis == "x" else [axis + "+", axis + "-"]
    return links


def shifted(off, link):
    dz, dy, dx = off
    dz += {"z+": -1, "z-": 1}.get(link, 0)
    dy += {"y+": -1, "y-": 1}.get(link, 0)
    dx ^= int(link == "x")
    return (4 if dz == -4 else dz, 2 if dy == -2 else dy, dx)


N_PLANES = 8
STEPS = 3 * N_PLANES
STARTS = (2, 0, 1)
START_US = (0.0, 4.2, 6.3)
CUTS = (0.5, 3.2, 4.7, 5.0, 6.8)


def plane_of(rank):
    return (rank + 1) // 2 * (1 - 2 * ((rank + 1) % 2))


def timetable(copy_us=1.65, hop_us=1.8, ahead_us=8.0):
    heap, count, queues, busy, arrived, served = [], 0, {}, {}, {}, []

    def put(now, what):
        nonlocal count
        count += 1
        heapq.heappush(heap, (now, count, what))

    def kick(link, now):
        if busy.get(link, 0.0) > now + 1e-6 or not queues.get(link):
            return
        _, _, color, off = heapq.heappop(queues[link])
        busy[link] = now + copy_us
        served.append((now, color, off, link))
        put(now + copy_us, (link,))
        put(now + copy_us + hop_us, (color, shifted(off, link), link))

    for color, start in zip(STARTS, START_US):
        put(start, (color, (0, 0, 0), "own"))
    while heap:
        now, order, what = heapq.heappop(heap)
        if len(what) == 1:
            kick(what[0], now)
            continue
        color, off, via = what
        arrived[color, off] = now
        for link in onward(color, off, via):
            count += 1
            heapq.heappush(queues.setdefault(link, []), (abs(off[0]), count, color, off))
            kick(link, now)
    actions = [(now, 0, one, None) for one, now in arrived.items() if one[1] != (0, 0, 0)]
    last = {}
    for start, color, off, link in served:
        due = max(arrived[color, off], start - ahead_us, last.get(link, 0.0))
        last[link] = due
        actions.append((due, 1, (color, off), link))
    actions.sort(key=lambda one: one[:2])
    return actions


def plan(step_us=1.7, first_us=1.5):
    actions = timetable()
    early = []
    for cut in CUTS:
        early.append([one for one in actions if one[0] <= cut])
        actions = actions[len(early[-1]) :]
    missing = []
    for unit in range(N_PLANES):
        dz = plane_of(unit)
        missing.append(
            {
                (color, (dz, dy, dx))
                for color in range(3)
                for dy in (0, 1, -1, 2)
                for dx in (0, 1)
                if (dz, dy, dx) != (0, 0, 0)
            }
        )
    taken = {one[2] for batch in early for one in batch if one[1] == 0}
    now, step, batches, batch = CUTS[-1] + first_us, 0, [], []
    while step < STEPS or actions:
        if actions and (actions[0][0] <= now or step == STEPS):
            one = actions.pop(0)
            if one[1] == 0:
                taken.add(one[2])
            now = max(now, one[0]) + 0.02
            batch.append(one)
        elif step < STEPS and missing[step // 3] <= taken:
            batches.append(batch)
            batch = []
            step += 1
            now += step_us
        else:
            now = actions[0][0]
    assert not batch
    return early, batches, now


EARLY, BATCHES, _ = plan()
OFFSETS = sorted({one[2][1] for batch in EARLY + BATCHES for one in batch if one[1] == 0})


def places():
    seq = lax.axis_index("seq")
    tp = lax.axis_index("tp")
    return seq // 8, (seq // 2) % 4, seq % 2, tp // 2, tp % 2


def seq_of(z, y, x_lo):
    return z * 8 + y * 2 + x_lo


def x_neighbours():
    z, y, x_lo, x_hi, core = places()
    x = x_hi * 2 + x_lo
    ids = []
    for step in (1, 3):
        other = lax.rem(x + step, 4)
        ids.append((seq_of(z, y, other % 2), (other // 2) * 2 + core))
    return x, ids


def greet(ids):
    barrier = pltpu.get_barrier_semaphore()
    for one in ids:
        pl.semaphore_signal(barrier, inc=1, device_id=one, device_id_type=MESH)
    pl.semaphore_wait(barrier, len(ids))


def remote(src, dst, send, recv, target):
    return pltpu.make_async_remote_copy(
        src_ref=src, dst_ref=dst, send_sem=send, recv_sem=recv, device_id=target,
        device_id_type=MESH,
    )


CHUNKS = 6
CHUNK = BLOCK // CHUNKS
SLOTS = N_SEQ // N_PLANES
KEYS = SLOTS * BLOCK
PIECES = 2
PIECE = KEYS // PIECES
QUERIES = GROUP * BLOCK
LAST_BLOCK = 2 * N_SEQ - 1
KV_COLS = 2 * HD


def layer_kernel(
    short_lengths, hidden, gain, frequency, page_slot, wq, wk, wv, w_out, out, pages,
    xbuf, relay, wbuf, wout, fbuf, total, cosine, sine, first_b, q, kv, buf, m_ref, l_ref, acc_ref,
    attended, sendp, recvp, sendx, recvx, relay_out,
    load_sem, send_sem, r0, r1, r2, r3, own_sem, seq_send, seq_recv, out_send, rp, o1, o2,
):
    z, y, x_lo, x_hi, core = places()
    seq = lax.axis_index("seq")
    tp = lax.axis_index("tp")
    loads = [
        pltpu.make_async_copy(hidden, xbuf.at[tp], load_sem.at[0]),
        pltpu.make_async_copy(wk, wbuf.at[:, 0:HD], load_sem.at[1]),
        pltpu.make_async_copy(wv, wbuf.at[:, HD:KV_COLS], load_sem.at[2]),
        pltpu.make_async_copy(wq, wbuf.at[:, KV_COLS:], load_sem.at[3]),
        pltpu.make_async_copy(frequency, fbuf, load_sem.at[4]),
        pltpu.make_async_copy(w_out, wout, load_sem.at[5]),
    ]
    for one in loads:
        one.start()
    x, sides = x_neighbours()
    partner = (seq, x_hi * 2 + 1 - core)
    target = {
        "x": (seq_of(z, y, 1 - x_lo), tp),
        "y+": (seq_of(z, lax.rem(y + 1, 4), x_lo), tp),
        "y-": (seq_of(z, lax.rem(y + 3, 4), x_lo), tp),
        "z+": (seq_of(lax.rem(z + 1, 8), y, x_lo), tp),
        "z-": (seq_of(lax.rem(z + 7, 8), y, x_lo), tp),
    }
    greet([partner] + sides + [target[link] for link in ("y+", "y-", "z+", "z-")])

    sends = []

    def go(copy):
        copy.start()
        sends.append(copy)
        return copy

    def rows_of(k):
        return pl.ds(k * CHUNK, CHUNK)

    def in_start_order(c):
        return STARTS[c // 2] * 2 + c % 2

    opposite = (1 - x_hi) * 2 + core
    loads[0].wait()
    firsts = {}

    def start_own(c):
        for way in range(2):
            k = way * CHUNKS + in_start_order(c)
            firsts[k] = go(
                remote(xbuf.at[tp, rows_of(k)], relay.at[k], send_sem.at[k], r1.at[k], sides[way])
            )

    for c in range(3):
        start_own(c)
    own = go(remote(xbuf.at[tp], xbuf.at[tp], send_sem.at[6 * CHUNKS], r0, partner))

    def pass_on(k):
        way = k // CHUNKS
        firsts[k].wait_recv()
        source = lax.rem(x + (3 if way == 0 else 1), 4)
        go(
            remote(
                relay.at[k], xbuf.at[(source // 2) * 2 + core, rows_of(k)],
                send_sem.at[2 * CHUNKS + k], r2.at[k], sides[way],
            )
        )

    thirds = {}

    def share(k):
        here = xbuf.at[opposite, rows_of(k)]
        remote(
            relay.at[k], here, send_sem.at[2 * CHUNKS + k], r2.at[k], sides[k // CHUNKS]
        ).wait_recv()
        thirds[k] = go(remote(here, here, send_sem.at[4 * CHUNKS + k], r3.at[k], partner))

    def weighted(wide, part):
        cols = pl.ds(pl.multiple_of(part * COLS, COLS), COLS)
        return (wide * gain[cols].astype(F32)[None, :]).astype(BF16), cols

    def whole_part(part, first):
        wide = xbuf[part].astype(F32)
        squares = jnp.sum(wide * wide, axis=1, keepdims=True)
        rows, cols = weighted(wide, part)
        product = jnp.dot(rows, wbuf[cols, :], preferred_element_type=F32)
        total[...] = product if first else total[...] + product
        return squares

    def lane_row(shape):
        lane = lax.broadcasted_iota(jnp.int32, shape, 1)
        return lane - BLOCK * sum((lane >= n * BLOCK).astype(jnp.int32) for n in range(1, GROUP))

    def facts():
        row = lax.broadcasted_iota(jnp.int32, (BLOCK, HD), 0)
        lane = lax.broadcasted_iota(jnp.int32, (BLOCK, HD), 1)
        sign = jnp.where(lane < HD // 2, -1.0, 1.0).astype(F32)
        for half in range(2):
            pos = row + (seq if half == 0 else LAST_BLOCK - seq) * BLOCK
            first = jnp.zeros((BLOCK, HD), jnp.int32)
            bound = LONG
            for j in range(short_lengths.shape[0]):
                first = jnp.where(pos >= bound, bound, first)
                bound = bound + short_lengths[j]
            angles = (pos - first).astype(F32) * fbuf[...]
            cosine[half] = jnp.cos(angles)
            sine[half] = jnp.sin(angles) * sign
        pos = lane_row((1, QUERIES)) + (LAST_BLOCK - seq) * BLOCK
        first = jnp.zeros((1, QUERIES), jnp.int32)
        bound = LONG
        for j in range(short_lengths.shape[0]):
            first = jnp.where(pos >= bound, bound, first)
            bound = bound + short_lengths[j]
        first_b[...] = first

    at_z = {dz: lax.rem(z + (dz + 8), 8) * 8 for dz in range(-3, 5)}
    at_y = {dy: lax.rem(y + (dy + 4), 4) * 2 for dy in range(-1, 3)}
    at_x = (x_lo, 1 - x_lo)
    at_yx = {(dy, dx): at_y[dy] + at_x[dx] for dy in at_y for dx in range(2)}

    def chunk(color, off):
        dz, dy, dx = off
        return buf.at[:, at_z[dz] + at_yx[dy, dx], color]

    def send(color, off, link, src):
        there = shifted(off, link)
        remote(
            src, chunk(color, off), seq_send.at[color],
            seq_recv.at[color, OFFSETS.index(there)], target[link],
        ).start()

    def take(batch):
        for _, sends_it, (color, off), link in batch:
            here = chunk(color, off)
            if not sends_it:
                remote(
                    here, here, seq_send.at[color], seq_recv.at[color, OFFSETS.index(off)],
                    target["x"],
                ).wait_recv()
            elif off == (0, 0, 0):
                send(color, off, link, kv.at[:, color])
            else:
                send(color, off, link, here)

    def own_copy(color):
        return pltpu.make_async_copy(kv.at[:, color], buf.at[:, seq, color], own_sem.at[color])

    far_parts = (opposite, (1 - x_hi) * 2 + 1 - core)

    def third(color):
        spans = [slice(half * BLOCK + color * THIRD, half * BLOCK + (color + 1) * THIRD)
                 for half in range(2)]
        for k in (2 * color, 2 * color + 1):
            for way in range(2):
                thirds[way * CHUNKS + k].wait_recv()
        sums = jnp.concatenate([squares[span] for span in spans])
        product = jnp.concatenate([total[span, :KV_COLS] for span in spans])
        kept = []
        for part in far_parts:
            wide = jnp.concatenate([xbuf[part, span] for span in spans]).astype(F32)
            sums = sums + jnp.sum(wide * wide, axis=1, keepdims=True)
            rows, cols = weighted(wide, part)
            kept.append(rows)
            product = product + jnp.dot(
                rows, wbuf[cols, :KV_COLS], preferred_element_type=F32
            )
        factor = lax.rsqrt(sums * (1.0 / D) + norm_eps)
        product = product * factor
        u = product[:, :HD]
        turned_u = pltpu.roll(u, HD // 2, 1)
        for half in range(2):
            rows = slice(half * THIRD, (half + 1) * THIRD)
            angle = slice(color * THIRD, (color + 1) * THIRD)
            kv[half, color] = (
                u[rows] * cosine[half, angle] + turned_u[rows] * sine[half, angle]
            ).astype(BF16)
            kv[2 + half, color] = product[rows, HD:].astype(BF16)
        own_copy(color).start()
        return kept, factor

    for one in loads[1:5]:
        one.wait()
    squares = whole_part(tp, True)
    late = []
    def both(do, c):
        for way in range(2):
            do(way * CHUNKS + in_start_order(c))

    both(pass_on, 0)
    start_own(3)
    own.wait_recv()
    squares = squares + whole_part(x_hi * 2 + 1 - core, False)
    both(pass_on, 1)
    start_own(4)
    both(pass_on, 2)
    start_own(5)
    facts()
    both(share, 0)
    both(pass_on, 3)
    both(share, 1)
    both(pass_on, 4)
    late.append(third(STARTS[0]))
    take(EARLY[0])
    both(share, 2)
    both(pass_on, 5)
    both(share, 3)
    both(share, 4)
    take(EARLY[1])
    late.append(third(STARTS[1]))
    take(EARLY[2])
    both(share, 5)
    take(EARLY[3])
    late.append(third(STARTS[2]))
    take(EARLY[4])
    for n, part in enumerate(far_parts):
        cols = pl.ds(pl.multiple_of(part * COLS, COLS), COLS)
        product = jnp.dot(
            jnp.concatenate([kept[n] for kept, _ in late]), wbuf[cols, KV_COLS:],
            preferred_element_type=F32,
        )
        for at, color in enumerate(STARTS):
            for half in range(2):
                first = half * BLOCK + color * THIRD
                there = (2 * at + half) * THIRD
                total[first : first + THIRD, KV_COLS:] += product[there : there + THIRD]
    for half in range(2):
        factor = jnp.concatenate(
            [late[STARTS.index(color)][1][half * THIRD : (half + 1) * THIRD] for color in range(3)]
        )
        for head in range(GROUP):
            u = total[
                half * BLOCK : (half + 1) * BLOCK,
                KV_COLS + head * HD : KV_COLS + (head + 1) * HD,
            ] * factor
            q[half, head * BLOCK : (head + 1) * BLOCK] = (
                u * cosine[half] + pltpu.roll(u, HD // 2, 1) * sine[half]
            ).astype(BF16)
    m_ref[...] = jnp.full(m_ref.shape, NEG, F32)
    l_ref[...] = jnp.zeros(l_ref.shape, F32)
    acc_ref[...] = jnp.zeros(acc_ref.shape, F32)
    for color in range(3):
        own_copy(color).wait()

    def step(half, region, plane, allowed):
        slots = pl.ds(plane * SLOTS, SLOTS)
        keys = buf[region, slots].reshape(KEYS, HD)
        values = buf[2 + region, slots].reshape(KEYS, HD)
        queries = q[half]
        pieces = [slice(n * PIECE, (n + 1) * PIECE) for n in range(PIECES)]
        scores = []
        for n, piece in enumerate(pieces):
            one = lax.dot_general(
                keys[piece], queries, (((1,), (1,)), ((), ())), preferred_element_type=F32
            )
            scores.append(one if allowed is None else jnp.where(allowed(n), one, NEG))
        old = m_ref[half]
        new = old
        for one in scores:
            new = jnp.maximum(new, jnp.max(one, axis=0, keepdims=True))
        shift = new * SCALE2
        keep = jnp.exp2(old * SCALE2 - shift)
        m_ref[half] = new
        denominator = l_ref[half] * keep
        numerator = acc_ref[half] * keep
        for n, piece in enumerate(pieces):
            weights = jnp.exp2(scores[n] * SCALE2 - shift)
            if allowed is not None:
                weights = jnp.where(allowed(n), weights, 0.0)
            denominator = denominator + jnp.sum(weights, axis=0, keepdims=True)
            numerator = numerator + lax.dot_general(
                values[piece], weights.astype(BF16), (((0,), (0,)), ((), ())),
                preferred_element_type=F32,
            )
        l_ref[half] = denominator
        acc_ref[half] = numerator

    def masked_a(plane):
        def allowed(n):
            key = lax.broadcasted_iota(jnp.int32, (PIECE, 1), 0) + (n * PIECE + plane * KEYS)
            return key <= lane_row((1, QUERIES)) + seq * BLOCK

        step(0, 0, plane, allowed)

    def masked_b(plane):
        def allowed(n):
            row = lax.broadcasted_iota(jnp.int32, (PIECE, 1), 0) + n * PIECE
            slot_in = sum((row >= k * BLOCK).astype(jnp.int32) for k in range(1, SLOTS))
            key = row - 2 * BLOCK * slot_in + (LAST_BLOCK - plane * SLOTS) * BLOCK
            query = lane_row((1, QUERIES)) + (LAST_BLOCK - seq) * BLOCK
            return (key <= query) & (key >= first_b[...])

        step(1, 1, plane, allowed)

    in_long = (seq + (LONG_BLOCKS - N_SEQ)) // N_SEQ

    def batch_at(unit, part):
        for k in range(N_PLANES):
            batch = BATCHES[3 * k + part]
            if batch:
                pl.when(unit == k)(functools.partial(take, batch))

    def finish(half):
        ready = jnp.transpose(acc_ref[half] / l_ref[half]).astype(BF16)
        for head in range(GROUP):
            attended[half * BLOCK : (half + 1) * BLOCK, head * HD : (head + 1) * HD] = ready[
                head * BLOCK : (head + 1) * BLOCK
            ]

    far = (1 - x_hi) * 2
    near = x_hi * 2

    def terms(part, half):
        cols = pl.ds(pl.multiple_of(part * COLS, COLS), COLS)
        return jnp.dot(
            attended[half * BLOCK : (half + 1) * BLOCK, :], wout[:, cols],
            preferred_element_type=F32,
        )

    def partner_copy(which, half):
        rows = pl.ds(half * BLOCK, BLOCK)
        k = 2 * which + half
        return remote(
            sendp.at[which, rows], recvp.at[which, rows], out_send.at[4 * CHUNKS + k], rp.at[k],
            partner,
        )

    def to_partner(which, half, part):
        sendp[which, pl.ds(half * BLOCK, BLOCK)] = terms(part, half).astype(BF16)
        partner_copy(which, half).start()

    def hop(k):
        return remote(
            sendx.at[rows_of(k)], relay_out.at[k], out_send.at[k], o1.at[k], sides[k % 2]
        )

    def land(k):
        return remote(
            relay_out.at[k], recvx.at[rows_of(k)], out_send.at[2 * CHUNKS + k], o2.at[k],
            sides[k % 2],
        )

    def chunks_of(half):
        return range(half * CHUNKS, (half + 1) * CHUNKS)

    def cross(half, mine):
        rows = pl.ds(half * BLOCK, BLOCK)
        partner_copy(0, half).wait_recv()
        sendx[rows] = (mine + recvp[0, rows].astype(F32)).astype(BF16)
        for k in chunks_of(half):
            hop(k).start()

    loads[5].wait()

    @pl.loop(0, N_PLANES)
    def _(unit):
        dz = (unit + 1) // 2 * (1 - 2 * ((unit + 1) % 2))
        plane = (z + dz + 8) % 8
        batch_at(unit, 0)

        @pl.when(plane < z)
        def _():
            step(0, 0, plane, None)

        @pl.when(plane == z)
        def _():
            masked_a(plane)

        @pl.when(unit == N_PLANES - 1)
        def _():
            finish(0)
            to_partner(0, 0, far + 1 - core)

        batch_at(unit, 1)

        @pl.when(in_long == 1)
        def _():
            step(1, 0, plane, None)

        @pl.when(unit == N_PLANES - 1)
        def _():
            cross(0, terms(far + core, 0))

        batch_at(unit, 2)

        @pl.when((in_long == 1) & (plane > z))
        def _():
            step(1, 1, plane, None)

        @pl.when((plane == z) | ((in_long == 0) & (plane == z + 1)))
        def _():
            masked_b(plane)

    finish(1)
    to_partner(0, 1, far + 1 - core)
    mine = terms(far + core, 1)
    for half in range(2):
        to_partner(1, half, near + 1 - core)
    cross(1, mine)
    for k in chunks_of(0):
        hop(k).wait_recv()
        land(k).start()
    for page in range(ROWS // PAGE):
        ids = lax.broadcasted_iota(jnp.int32, page_slot.shape, 0) * page_slot.shape[
            1
        ] + lax.broadcasted_iota(jnp.int32, page_slot.shape, 1)
        name = jnp.max(jnp.where(page_slot[...] == seq * (ROWS // PAGE) + page, ids, 0))
        block = name // (BLOCK // PAGE)
        part = name - block * (BLOCK // PAGE)
        region = block // N_SEQ
        slot = block + region * (LAST_BLOCK - 2 * block)
        pages[page, 0] = buf[region, slot, part]
        pages[page, 1] = buf[region + 2, slot, part]
    for k in chunks_of(1):
        hop(k).wait_recv()
        land(k).start()
    own_x = xbuf[tp].astype(F32)
    for half in range(2):
        rows = slice(half * BLOCK, (half + 1) * BLOCK)
        kept = terms(near + core, half) + own_x[rows]
        partner_copy(1, half).wait_recv()
        kept = kept + recvp[1, rows].astype(F32)
        for k in chunks_of(half):
            land(k).wait_recv()
        out[rows, :] = (kept + recvx[rows].astype(F32)).astype(BF16)
    for one in sends:
        one.wait_send()
    for half in range(2):
        for which in range(2):
            partner_copy(which, half).wait_send()
        for k in chunks_of(half):
            hop(k).wait_send()
            land(k).wait_send()
    for color in range(3):
        sent = buf.at[:, pl.ds(0, N_SEQ - 1), color]
        pltpu.make_async_copy(sent, sent, seq_send.at[color]).wait()


VM = pl.BlockSpec(memory_space=pltpu.VMEM)
SM = pl.BlockSpec(memory_space=pltpu.SMEM)
ANY = pl.BlockSpec(memory_space=pl.ANY)
DMA = pltpu.SemaphoreType.DMA


def in_hbm(one):
    return pltpu.with_memory_space_constraint(one, pltpu.HBM)


def local(hidden_in, norm_gain, w_query, w_key, w_value, w_out, short_lengths, page_slot):
    half = np.arange(HD // 2, dtype=np.float32)
    frequency = np.float32(rope_base) ** (-(half * np.float32(2.0)) / np.float32(HD))
    frequency = np.concatenate([frequency, frequency]).astype(np.float32).reshape(1, HD)
    return pl.pallas_call(
        layer_kernel,
        out_shape=(
            jax.ShapeDtypeStruct((ROWS, COLS), BF16),
            jax.ShapeDtypeStruct((ROWS // PAGE, 2, PAGE, HD), BF16),
        ),
        in_specs=[SM, ANY, VM, ANY, VM, ANY, ANY, ANY, ANY],
        out_specs=(VM, VM),
        scratch_shapes=[
            pltpu.VMEM((N_TP, ROWS, COLS), BF16),
            pltpu.VMEM((2 * CHUNKS, CHUNK, COLS), BF16),
            pltpu.VMEM((D, KV_COLS + HEAD_COLS), BF16),
            pltpu.VMEM((HEAD_COLS, D), BF16),
            pltpu.VMEM((1, HD), F32),
            pltpu.VMEM((ROWS, KV_COLS + HEAD_COLS), F32),
            pltpu.VMEM((2, BLOCK, HD), F32),
            pltpu.VMEM((2, BLOCK, HD), F32),
            pltpu.VMEM((1, QUERIES), jnp.int32),
            pltpu.VMEM((2, QUERIES, HD), BF16),
            pltpu.VMEM((4, BLOCK // THIRD, THIRD, HD), BF16),
            pltpu.VMEM((4, N_SEQ, BLOCK // THIRD, THIRD, HD), BF16),
            pltpu.VMEM((2, 1, QUERIES), F32),
            pltpu.VMEM((2, 1, QUERIES), F32),
            pltpu.VMEM((2, HD, QUERIES), F32),
            pltpu.VMEM((ROWS, HEAD_COLS), BF16),
            pltpu.VMEM((2, ROWS, COLS), BF16),
            pltpu.VMEM((2, ROWS, COLS), BF16),
            pltpu.VMEM((ROWS, COLS), BF16),
            pltpu.VMEM((ROWS, COLS), BF16),
            pltpu.VMEM((2 * CHUNKS, CHUNK, COLS), BF16),
            DMA((6,)),
            DMA((6 * CHUNKS + 1,)),
            DMA(()),
            DMA((2 * CHUNKS,)),
            DMA((2 * CHUNKS,)),
            DMA((2 * CHUNKS,)),
            DMA((3,)),
            DMA((3,)),
            DMA((3, len(OFFSETS))),
            DMA((4 * CHUNKS + 4,)),
            DMA((4,)),
            DMA((2 * CHUNKS,)),
            DMA((2 * CHUNKS,)),
        ],
        compiler_params=pltpu.CompilerParams(
            collective_id=0, has_side_effects=True, vmem_limit_bytes=44 * 1024 * 1024
        ),
        name="layer",
    )(*(in_hbm(one) for one in (
        short_lengths,
        hidden_in,
        norm_gain,
        jnp.asarray(frequency),
        page_slot.reshape(-1, HD),
        w_query,
        w_key,
        w_value,
        w_out,
    )))


def solution(mesh):
    placed = (
        P("seq", "tp"),
        P(),
        P(None, "tp"),
        P(None, "tp"),
        P(None, "tp"),
        P("tp", None),
        P(),
        P(),
    )
    return jax.shard_map(
        local,
        mesh=mesh,
        in_specs=placed,
        out_specs=(P("seq", "tp"), P("seq", None, None, "tp")),
        check_vma=False,
    )
```

```python
import functools
import heapq
import math

import jax
import jax.numpy as jnp
import numpy as np
from jax import lax
from jax.experimental import pallas as pl
from jax.experimental.pallas import tpu as pltpu
from jax.sharding import PartitionSpec as P

MESH = pl.DeviceIdType.MESH
F32 = jnp.float32
BF16 = jnp.bfloat16

D = 3072
QH = 12
KVH = 4
HD = 128
PAGE = 64
GROUP = 3
N_SEQ = 64
N_TP = 4
ROWS = 384
BLOCK = 192
COLS = D // N_TP
HEAD_COLS = GROUP * HD
LONG = 16512
LONG_BLOCKS = LONG // BLOCK
THIRD = 64
rope_base = 500000.0
norm_eps = 1e-05
SCALE2 = math.log2(math.e) / math.sqrt(HD)
NEG = -1e30


def onward(color, off, via):
    dz, dy, dx = off
    order = ("xyz", "xzy", "zyx")[color]
    if via == "own":
        links = []
        for axis in order:
            links += ["x"] if axis == "x" else [axis + "+", axis + "-"]
        return links
    links = []
    if via == "z+" and (dz in (-1, -2) or (dz == -3 and (color == 2 or dx == 0))):
        links.append(via)
    if via == "z-" and (dz in (1, 2) or (dz == 3 and color != 2 and dx == 1)):
        links.append(via)
    if via == "y+" and dy == -1 and (dz % 2 == 0 if color == 2 else dx == 0):
        links.append(via)
    if via == "y-" and dy == 1 and (dz % 2 == 1 if color == 2 else dx == 1):
        links.append(via)
    for axis in order[order.index(via[0]) + 1 :]:
        links += ["x"] if axis == "x" else [axis + "+", axis + "-"]
    return links


def shifted(off, link):
    dz, dy, dx = off
    dz += {"z+": -1, "z-": 1}.get(link, 0)
    dy += {"y+": -1, "y-": 1}.get(link, 0)
    dx ^= int(link == "x")
    return (4 if dz == -4 else dz, 2 if dy == -2 else dy, dx)


N_PLANES = 8
STEPS = 3 * N_PLANES
STARTS = (2, 0, 1)
START_US = (0.0, 4.2, 6.3)
CUTS = (0.5, 3.2, 4.7, 5.0, 6.8)


def plane_of(rank):
    return (rank + 1) // 2 * (1 - 2 * ((rank + 1) % 2))


def timetable(copy_us=1.65, hop_us=1.9, ahead_us=8.0):
    heap, count, queues, busy, arrived, served = [], 0, {}, {}, {}, []

    def put(now, what):
        nonlocal count
        count += 1
        heapq.heappush(heap, (now, count, what))

    def kick(link, now):
        if busy.get(link, 0.0) > now + 1e-6 or not queues.get(link):
            return
        _, _, color, off = heapq.heappop(queues[link])
        busy[link] = now + copy_us
        served.append((now, color, off, link))
        put(now + copy_us, (link,))
        put(now + copy_us + hop_us, (color, shifted(off, link), link))

    for color, start in zip(STARTS, START_US):
        put(start, (color, (0, 0, 0), "own"))
    while heap:
        now, order, what = heapq.heappop(heap)
        if len(what) == 1:
            kick(what[0], now)
            continue
        color, off, via = what
        arrived[color, off] = now
        for link in onward(color, off, via):
            count += 1
            heapq.heappush(queues.setdefault(link, []), (abs(off[0]), count, color, off))
            kick(link, now)
    actions = [(now, 0, one, None) for one, now in arrived.items() if one[1] != (0, 0, 0)]
    last = {}
    for start, color, off, link in served:
        due = max(arrived[color, off], start - ahead_us, last.get(link, 0.0))
        last[link] = due
        actions.append((due, 1, (color, off), link))
    actions.sort(key=lambda one: one[:2])
    return actions


def plan(step_us=1.6, first_us=1.5):
    actions = timetable()
    early = []
    for cut in CUTS:
        early.append([one for one in actions if one[0] <= cut])
        actions = actions[len(early[-1]) :]
    missing = []
    for unit in range(N_PLANES):
        dz = plane_of(unit)
        missing.append(
            {
                (color, (dz, dy, dx))
                for color in range(3)
                for dy in (0, 1, -1, 2)
                for dx in (0, 1)
                if (dz, dy, dx) != (0, 0, 0)
            }
        )
    taken = {one[2] for batch in early for one in batch if one[1] == 0}
    now, step, batches, batch = CUTS[-1] + first_us, 0, [], []
    while step < STEPS or actions:
        if actions and (actions[0][0] <= now or step == STEPS):
            one = actions.pop(0)
            if one[1] == 0:
                taken.add(one[2])
            now = max(now, one[0]) + 0.02
            batch.append(one)
        elif step < STEPS and missing[step // 3] <= taken:
            batches.append(batch)
            batch = []
            step += 1
            now += step_us
        else:
            now = actions[0][0]
    assert not batch
    return early, batches, now


EARLY, BATCHES, _ = plan()
OFFSETS = sorted({one[2][1] for batch in EARLY + BATCHES for one in batch if one[1] == 0})


def places():
    seq = lax.axis_index("seq")
    tp = lax.axis_index("tp")
    return seq // 8, (seq // 2) % 4, seq % 2, tp // 2, tp % 2


def seq_of(z, y, x_lo):
    return z * 8 + y * 2 + x_lo


def x_neighbours():
    z, y, x_lo, x_hi, core = places()
    x = x_hi * 2 + x_lo
    ids = []
    for step in (1, 3):
        other = lax.rem(x + step, 4)
        ids.append((seq_of(z, y, other % 2), (other // 2) * 2 + core))
    return x, ids


def greet(ids):
    barrier = pltpu.get_barrier_semaphore()
    for one in ids:
        pl.semaphore_signal(barrier, inc=1, device_id=one, device_id_type=MESH)
    pl.semaphore_wait(barrier, len(ids))


def remote(src, dst, send, recv, target):
    return pltpu.make_async_remote_copy(
        src_ref=src, dst_ref=dst, send_sem=send, recv_sem=recv, device_id=target,
        device_id_type=MESH,
    )


CHUNKS = 6
CHUNK = BLOCK // CHUNKS
SLOTS = N_SEQ // N_PLANES
KEYS = SLOTS * BLOCK
PIECES = 2
PIECE = KEYS // PIECES
QUERIES = GROUP * BLOCK
LAST_BLOCK = 2 * N_SEQ - 1
KV_COLS = 2 * HD


def layer_kernel(
    short_lengths, hidden, gain, frequency, page_slot, wq, wk, wv, w_out, out, pages,
    xbuf, relay, wbuf, wout, fbuf, total, cosine, sine, first_b, q, kv, buf, m_ref, l_ref, acc_ref,
    attended, sendp, recvp, sendx, recvx, relay_out,
    load_sem, send_sem, r0, r1, r2, r3, own_sem, seq_send, seq_recv, out_send, rp, o1, o2,
):
    z, y, x_lo, x_hi, core = places()
    seq = lax.axis_index("seq")
    tp = lax.axis_index("tp")
    loads = [
        pltpu.make_async_copy(hidden, xbuf.at[tp], load_sem.at[0]),
        pltpu.make_async_copy(wk, wbuf.at[:, 0:HD], load_sem.at[1]),
        pltpu.make_async_copy(wv, wbuf.at[:, HD:KV_COLS], load_sem.at[2]),
        pltpu.make_async_copy(wq, wbuf.at[:, KV_COLS:], load_sem.at[3]),
        pltpu.make_async_copy(frequency, fbuf, load_sem.at[4]),
        pltpu.make_async_copy(w_out, wout, load_sem.at[5]),
    ]
    for one in loads:
        one.start()
    x, sides = x_neighbours()
    partner = (seq, x_hi * 2 + 1 - core)
    target = {
        "x": (seq_of(z, y, 1 - x_lo), tp),
        "y+": (seq_of(z, lax.rem(y + 1, 4), x_lo), tp),
        "y-": (seq_of(z, lax.rem(y + 3, 4), x_lo), tp),
        "z+": (seq_of(lax.rem(z + 1, 8), y, x_lo), tp),
        "z-": (seq_of(lax.rem(z + 7, 8), y, x_lo), tp),
    }
    greet([partner] + sides + [target[link] for link in ("y+", "y-", "z+", "z-")])

    sends = []

    def go(copy):
        copy.start()
        sends.append(copy)
        return copy

    def rows_of(k):
        return pl.ds(k * CHUNK, CHUNK)

    def in_start_order(c):
        return STARTS[c // 2] * 2 + c % 2

    opposite = (1 - x_hi) * 2 + core
    loads[0].wait()
    firsts = {}

    def start_own(c):
        for way in range(2):
            k = way * CHUNKS + in_start_order(c)
            firsts[k] = go(
                remote(xbuf.at[tp, rows_of(k)], relay.at[k], send_sem.at[k], r1.at[k], sides[way])
            )

    for c in range(3):
        start_own(c)
    own = go(remote(xbuf.at[tp], xbuf.at[tp], send_sem.at[6 * CHUNKS], r0, partner))

    def pass_on(k):
        way = k // CHUNKS
        firsts[k].wait_recv()
        source = lax.rem(x + (3 if way == 0 else 1), 4)
        go(
            remote(
                relay.at[k], xbuf.at[(source // 2) * 2 + core, rows_of(k)],
                send_sem.at[2 * CHUNKS + k], r2.at[k], sides[way],
            )
        )

    thirds = {}

    def share(k):
        here = xbuf.at[opposite, rows_of(k)]
        remote(
            relay.at[k], here, send_sem.at[2 * CHUNKS + k], r2.at[k], sides[k // CHUNKS]
        ).wait_recv()
        thirds[k] = go(remote(here, here, send_sem.at[4 * CHUNKS + k], r3.at[k], partner))

    def weighted(wide, part):
        cols = pl.ds(pl.multiple_of(part * COLS, COLS), COLS)
        return (wide * gain[cols].astype(F32)[None, :]).astype(BF16), cols

    def whole_part(part, first):
        wide = xbuf[part].astype(F32)
        squares = jnp.sum(wide * wide, axis=1, keepdims=True)
        rows, cols = weighted(wide, part)
        product = jnp.dot(rows, wbuf[cols, :], preferred_element_type=F32)
        total[...] = product if first else total[...] + product
        return squares

    def lane_row(shape):
        lane = lax.broadcasted_iota(jnp.int32, shape, 1)
        return lane - BLOCK * sum((lane >= n * BLOCK).astype(jnp.int32) for n in range(1, GROUP))

    def facts():
        row = lax.broadcasted_iota(jnp.int32, (BLOCK, HD), 0)
        lane = lax.broadcasted_iota(jnp.int32, (BLOCK, HD), 1)
        sign = jnp.where(lane < HD // 2, -1.0, 1.0).astype(F32)
        for half in range(2):
            pos = row + (seq if half == 0 else LAST_BLOCK - seq) * BLOCK
            first = jnp.zeros((BLOCK, HD), jnp.int32)
            bound = LONG
            for j in range(short_lengths.shape[0]):
                first = jnp.where(pos >= bound, bound, first)
                bound = bound + short_lengths[j]
            angles = (pos - first).astype(F32) * fbuf[...]
            cosine[half] = jnp.cos(angles)
            sine[half] = jnp.sin(angles) * sign
        pos = lane_row((1, QUERIES)) + (LAST_BLOCK - seq) * BLOCK
        first = jnp.zeros((1, QUERIES), jnp.int32)
        bound = LONG
        for j in range(short_lengths.shape[0]):
            first = jnp.where(pos >= bound, bound, first)
            bound = bound + short_lengths[j]
        first_b[...] = first

    at_z = {dz: lax.rem(z + (dz + 8), 8) * 8 for dz in range(-3, 5)}
    at_y = {dy: lax.rem(y + (dy + 4), 4) * 2 for dy in range(-1, 3)}
    at_x = (x_lo, 1 - x_lo)
    at_yx = {(dy, dx): at_y[dy] + at_x[dx] for dy in at_y for dx in range(2)}

    def chunk(color, off):
        dz, dy, dx = off
        return buf.at[:, at_z[dz] + at_yx[dy, dx], color]

    def send(color, off, link, src):
        there = shifted(off, link)
        remote(
            src, chunk(color, off), seq_send.at[color],
            seq_recv.at[color, OFFSETS.index(there)], target[link],
        ).start()

    def take(batch):
        for _, sends_it, (color, off), link in batch:
            here = chunk(color, off)
            if not sends_it:
                remote(
                    here, here, seq_send.at[color], seq_recv.at[color, OFFSETS.index(off)],
                    target["x"],
                ).wait_recv()
            elif off == (0, 0, 0):
                send(color, off, link, kv.at[:, color])
            else:
                send(color, off, link, here)

    def own_copy(color):
        return pltpu.make_async_copy(kv.at[:, color], buf.at[:, seq, color], own_sem.at[color])

    far_parts = (opposite, (1 - x_hi) * 2 + 1 - core)

    def third(color):
        spans = [slice(half * BLOCK + color * THIRD, half * BLOCK + (color + 1) * THIRD)
                 for half in range(2)]
        for k in (2 * color, 2 * color + 1):
            for way in range(2):
                thirds[way * CHUNKS + k].wait_recv()
        sums = jnp.concatenate([squares[span] for span in spans])
        product = jnp.concatenate([total[span, :KV_COLS] for span in spans])
        kept = []
        for part in far_parts:
            wide = jnp.concatenate([xbuf[part, span] for span in spans]).astype(F32)
            sums = sums + jnp.sum(wide * wide, axis=1, keepdims=True)
            rows, cols = weighted(wide, part)
            kept.append(rows)
            product = product + jnp.dot(
                rows, wbuf[cols, :KV_COLS], preferred_element_type=F32
            )
        factor = lax.rsqrt(sums * (1.0 / D) + norm_eps)
        product = product * factor
        u = product[:, :HD]
        turned_u = pltpu.roll(u, HD // 2, 1)
        for half in range(2):
            rows = slice(half * THIRD, (half + 1) * THIRD)
            angle = slice(color * THIRD, (color + 1) * THIRD)
            kv[half, color] = (
                u[rows] * cosine[half, angle] + turned_u[rows] * sine[half, angle]
            ).astype(BF16)
            kv[2 + half, color] = product[rows, HD:].astype(BF16)
        own_copy(color).start()
        return kept, factor

    for one in loads[1:5]:
        one.wait()
    squares = whole_part(tp, True)
    late = []
    def both(do, c):
        for way in range(2):
            do(way * CHUNKS + in_start_order(c))

    both(pass_on, 0)
    start_own(3)
    own.wait_recv()
    squares = squares + whole_part(x_hi * 2 + 1 - core, False)
    both(pass_on, 1)
    start_own(4)
    both(pass_on, 2)
    start_own(5)
    facts()
    both(share, 0)
    both(pass_on, 3)
    both(share, 1)
    both(pass_on, 4)
    late.append(third(STARTS[0]))
    take(EARLY[0])
    both(share, 2)
    both(pass_on, 5)
    both(share, 3)
    both(share, 4)
    take(EARLY[1])
    late.append(third(STARTS[1]))
    take(EARLY[2])
    both(share, 5)
    take(EARLY[3])
    late.append(third(STARTS[2]))
    take(EARLY[4])
    for n, part in enumerate(far_parts):
        cols = pl.ds(pl.multiple_of(part * COLS, COLS), COLS)
        product = jnp.dot(
            jnp.concatenate([kept[n] for kept, _ in late]), wbuf[cols, KV_COLS:],
            preferred_element_type=F32,
        )
        for at, color in enumerate(STARTS):
            for half in range(2):
                first = half * BLOCK + color * THIRD
                there = (2 * at + half) * THIRD
                total[first : first + THIRD, KV_COLS:] += product[there : there + THIRD]
    for half in range(2):
        factor = jnp.concatenate(
            [late[STARTS.index(color)][1][half * THIRD : (half + 1) * THIRD] for color in range(3)]
        )
        for head in range(GROUP):
            u = total[
                half * BLOCK : (half + 1) * BLOCK,
                KV_COLS + head * HD : KV_COLS + (head + 1) * HD,
            ] * factor
            q[half, head * BLOCK : (head + 1) * BLOCK] = (
                u * cosine[half] + pltpu.roll(u, HD // 2, 1) * sine[half]
            ).astype(BF16)
    m_ref[...] = jnp.full(m_ref.shape, NEG, F32)
    l_ref[...] = jnp.zeros(l_ref.shape, F32)
    acc_ref[...] = jnp.zeros(acc_ref.shape, F32)
    for color in range(3):
        own_copy(color).wait()

    def step(half, region, plane, allowed):
        slots = pl.ds(plane * SLOTS, SLOTS)
        keys = buf[region, slots].reshape(KEYS, HD)
        values = buf[2 + region, slots].reshape(KEYS, HD)
        queries = q[half]
        pieces = [slice(n * PIECE, (n + 1) * PIECE) for n in range(PIECES)]
        scores = []
        for n, piece in enumerate(pieces):
            one = lax.dot_general(
                keys[piece], queries, (((1,), (1,)), ((), ())), preferred_element_type=F32
            )
            scores.append(one if allowed is None else jnp.where(allowed(n), one, NEG))
        old = m_ref[half]
        new = old
        for one in scores:
            new = jnp.maximum(new, jnp.max(one, axis=0, keepdims=True))
        shift = new * SCALE2
        keep = jnp.exp2(old * SCALE2 - shift)
        m_ref[half] = new
        denominator = l_ref[half] * keep
        numerator = acc_ref[half] * keep
        for n, piece in enumerate(pieces):
            weights = jnp.exp2(scores[n] * SCALE2 - shift)
            if allowed is not None:
                weights = jnp.where(allowed(n), weights, 0.0)
            denominator = denominator + jnp.sum(weights, axis=0, keepdims=True)
            numerator = numerator + lax.dot_general(
                values[piece], weights.astype(BF16), (((0,), (0,)), ((), ())),
                preferred_element_type=F32,
            )
        l_ref[half] = denominator
        acc_ref[half] = numerator

    def masked_a(plane):
        def allowed(n):
            key = lax.broadcasted_iota(jnp.int32, (PIECE, 1), 0) + (n * PIECE + plane * KEYS)
            return key <= lane_row((1, QUERIES)) + seq * BLOCK

        step(0, 0, plane, allowed)

    def masked_b(plane):
        def allowed(n):
            row = lax.broadcasted_iota(jnp.int32, (PIECE, 1), 0) + n * PIECE
            slot_in = sum((row >= k * BLOCK).astype(jnp.int32) for k in range(1, SLOTS))
            key = row - 2 * BLOCK * slot_in + (LAST_BLOCK - plane * SLOTS) * BLOCK
            query = lane_row((1, QUERIES)) + (LAST_BLOCK - seq) * BLOCK
            return (key <= query) & (key >= first_b[...])

        step(1, 1, plane, allowed)

    in_long = (seq + (LONG_BLOCKS - N_SEQ)) // N_SEQ

    def batch_at(unit, part):
        for k in range(N_PLANES):
            batch = BATCHES[3 * k + part]
            if batch:
                pl.when(unit == k)(functools.partial(take, batch))

    def finish(half):
        ready = jnp.transpose(acc_ref[half] / l_ref[half]).astype(BF16)
        for head in range(GROUP):
            attended[half * BLOCK : (half + 1) * BLOCK, head * HD : (head + 1) * HD] = ready[
                head * BLOCK : (head + 1) * BLOCK
            ]

    far = (1 - x_hi) * 2
    near = x_hi * 2

    def terms(part, half):
        cols = pl.ds(pl.multiple_of(part * COLS, COLS), COLS)
        return jnp.dot(
            attended[half * BLOCK : (half + 1) * BLOCK, :], wout[:, cols],
            preferred_element_type=F32,
        )

    def partner_copy(which, half):
        rows = pl.ds(half * BLOCK, BLOCK)
        k = 2 * which + half
        return remote(
            sendp.at[which, rows], recvp.at[which, rows], out_send.at[4 * CHUNKS + k], rp.at[k],
            partner,
        )

    def to_partner(which, half, part):
        sendp[which, pl.ds(half * BLOCK, BLOCK)] = terms(part, half).astype(BF16)
        partner_copy(which, half).start()

    def hop(k):
        return remote(
            sendx.at[rows_of(k)], relay_out.at[k], out_send.at[k], o1.at[k], sides[k % 2]
        )

    def land(k):
        return remote(
            relay_out.at[k], recvx.at[rows_of(k)], out_send.at[2 * CHUNKS + k], o2.at[k],
            sides[k % 2],
        )

    def chunks_of(half):
        return range(half * CHUNKS, (half + 1) * CHUNKS)

    def cross(half, mine):
        rows = pl.ds(half * BLOCK, BLOCK)
        partner_copy(0, half).wait_recv()
        sendx[rows] = (mine + recvp[0, rows].astype(F32)).astype(BF16)
        for k in chunks_of(half):
            hop(k).start()

    loads[5].wait()

    @pl.loop(0, N_PLANES)
    def _(unit):
        dz = (unit + 1) // 2 * (1 - 2 * ((unit + 1) % 2))
        plane = (z + dz + 8) % 8
        batch_at(unit, 0)

        @pl.when(plane < z)
        def _():
            step(0, 0, plane, None)

        @pl.when(plane == z)
        def _():
            masked_a(plane)

        @pl.when(unit == N_PLANES - 1)
        def _():
            finish(0)
            to_partner(0, 0, far + 1 - core)

        batch_at(unit, 1)

        @pl.when(in_long == 1)
        def _():
            step(1, 0, plane, None)

        @pl.when(unit == N_PLANES - 1)
        def _():
            cross(0, terms(far + core, 0))

        batch_at(unit, 2)

        @pl.when((in_long == 1) & (plane > z))
        def _():
            step(1, 1, plane, None)

        @pl.when((plane == z) | ((in_long == 0) & (plane == z + 1)))
        def _():
            masked_b(plane)

    finish(1)
    to_partner(0, 1, far + 1 - core)
    mine = terms(far + core, 1)
    for half in range(2):
        to_partner(1, half, near + 1 - core)
    cross(1, mine)
    for k in chunks_of(0):
        hop(k).wait_recv()
        land(k).start()
    for page in range(ROWS // PAGE):
        ids = lax.broadcasted_iota(jnp.int32, page_slot.shape, 0) * page_slot.shape[
            1
        ] + lax.broadcasted_iota(jnp.int32, page_slot.shape, 1)
        name = jnp.max(jnp.where(page_slot[...] == seq * (ROWS // PAGE) + page, ids, 0))
        block = name // (BLOCK // PAGE)
        part = name - block * (BLOCK // PAGE)
        region = block // N_SEQ
        slot = block + region * (LAST_BLOCK - 2 * block)
        pages[page, 0] = buf[region, slot, part]
        pages[page, 1] = buf[region + 2, slot, part]
    for k in chunks_of(1):
        hop(k).wait_recv()
        land(k).start()
    own_x = xbuf[tp].astype(F32)
    for half in range(2):
        rows = slice(half * BLOCK, (half + 1) * BLOCK)
        kept = terms(near + core, half) + own_x[rows]
        partner_copy(1, half).wait_recv()
        kept = kept + recvp[1, rows].astype(F32)
        for k in chunks_of(half):
            land(k).wait_recv()
        out[rows, :] = (kept + recvx[rows].astype(F32)).astype(BF16)
    for one in sends:
        one.wait_send()
    for half in range(2):
        for which in range(2):
            partner_copy(which, half).wait_send()
        for k in chunks_of(half):
            hop(k).wait_send()
            land(k).wait_send()
    for color in range(3):
        sent = buf.at[:, pl.ds(0, N_SEQ - 1), color]
        pltpu.make_async_copy(sent, sent, seq_send.at[color]).wait()


VM = pl.BlockSpec(memory_space=pltpu.VMEM)
SM = pl.BlockSpec(memory_space=pltpu.SMEM)
ANY = pl.BlockSpec(memory_space=pl.ANY)
DMA = pltpu.SemaphoreType.DMA


def in_hbm(one):
    return pltpu.with_memory_space_constraint(one, pltpu.HBM)


def local(hidden_in, norm_gain, w_query, w_key, w_value, w_out, short_lengths, page_slot):
    half = np.arange(HD // 2, dtype=np.float32)
    frequency = np.float32(rope_base) ** (-(half * np.float32(2.0)) / np.float32(HD))
    frequency = np.concatenate([frequency, frequency]).astype(np.float32).reshape(1, HD)
    return pl.pallas_call(
        layer_kernel,
        out_shape=(
            jax.ShapeDtypeStruct((ROWS, COLS), BF16),
            jax.ShapeDtypeStruct((ROWS // PAGE, 2, PAGE, HD), BF16),
        ),
        in_specs=[SM, ANY, VM, ANY, VM, ANY, ANY, ANY, ANY],
        out_specs=(VM, VM),
        scratch_shapes=[
            pltpu.VMEM((N_TP, ROWS, COLS), BF16),
            pltpu.VMEM((2 * CHUNKS, CHUNK, COLS), BF16),
            pltpu.VMEM((D, KV_COLS + HEAD_COLS), BF16),
            pltpu.VMEM((HEAD_COLS, D), BF16),
            pltpu.VMEM((1, HD), F32),
            pltpu.VMEM((ROWS, KV_COLS + HEAD_COLS), F32),
            pltpu.VMEM((2, BLOCK, HD), F32),
            pltpu.VMEM((2, BLOCK, HD), F32),
            pltpu.VMEM((1, QUERIES), jnp.int32),
            pltpu.VMEM((2, QUERIES, HD), BF16),
            pltpu.VMEM((4, BLOCK // THIRD, THIRD, HD), BF16),
            pltpu.VMEM((4, N_SEQ, BLOCK // THIRD, THIRD, HD), BF16),
            pltpu.VMEM((2, 1, QUERIES), F32),
            pltpu.VMEM((2, 1, QUERIES), F32),
            pltpu.VMEM((2, HD, QUERIES), F32),
            pltpu.VMEM((ROWS, HEAD_COLS), BF16),
            pltpu.VMEM((2, ROWS, COLS), BF16),
            pltpu.VMEM((2, ROWS, COLS), BF16),
            pltpu.VMEM((ROWS, COLS), BF16),
            pltpu.VMEM((ROWS, COLS), BF16),
            pltpu.VMEM((2 * CHUNKS, CHUNK, COLS), BF16),
            DMA((6,)),
            DMA((6 * CHUNKS + 1,)),
            DMA(()),
            DMA((2 * CHUNKS,)),
            DMA((2 * CHUNKS,)),
            DMA((2 * CHUNKS,)),
            DMA((3,)),
            DMA((3,)),
            DMA((3, len(OFFSETS))),
            DMA((4 * CHUNKS + 4,)),
            DMA((4,)),
            DMA((2 * CHUNKS,)),
            DMA((2 * CHUNKS,)),
        ],
        compiler_params=pltpu.CompilerParams(
            collective_id=0, has_side_effects=True, vmem_limit_bytes=44 * 1024 * 1024
        ),
        name="layer",
    )(*(in_hbm(one) for one in (
        short_lengths,
        hidden_in,
        norm_gain,
        jnp.asarray(frequency),
        page_slot.reshape(-1, HD),
        w_query,
        w_key,
        w_value,
        w_out,
    )))


def solution(mesh):
    placed = (
        P("seq", "tp"),
        P(),
        P(None, "tp"),
        P(None, "tp"),
        P(None, "tp"),
        P("tp", None),
        P(),
        P(),
    )
    return jax.shard_map(
        local,
        mesh=mesh,
        in_specs=placed,
        out_specs=(P("seq", "tp"), P("seq", None, None, "tp")),
        check_vma=False,
    )
```
